768 devices in a mesh: seq: 32 (over x, y_hi, core), tp: 24 (over z, y_lo).
Axes of the slice: x: 4, y: 8 (y_hi: 4, y_lo: 2; y = y_hi * 2 + y_lo), z: 12, core: 2. Of those that a mesh axis runs over, the one named last changes fastest.
Arguments:
- queries: bfloat16 [16384, 6144], P('seq', 'tp'), may hold values from -6 to 6
- cotangent: bfloat16 [16384, 6144], P('seq', 'tp'), may hold values from -6 to 6
- gate: float32 [48], P('tp'), may hold values from 0.2 to 1.5
- token_image: int32 [16384], P('seq'), may hold values from 0 to 32, as said below
- patches: bfloat16 [32, 256, 1280], P('seq'), may hold values from -6 to 6
- patch_count: int32 [32], P('seq'), may hold values from 0 to 256, as said below
- latents: bfloat16 [64, 1280], replicated, may hold values from -6 to 6
- latent_queries: bfloat16 [64, 768], replicated, may hold values from -6 to 6
- rs_key: bfloat16 [1280, 768], replicated, may hold values from -0.15625 to 0.15625
- rs_value: bfloat16 [1280, 768], replicated, may hold values from -0.15625 to 0.15625
- rs_out: bfloat16 [768, 1280], replicated, may hold values from -0.21875 to 0.21875
- key_weight: bfloat16 [1280, 6144], P(None, 'tp'), may hold values from -0.15625 to 0.15625
- value_weight: bfloat16 [1280, 6144], P(None, 'tp'), may hold values from -0.15625 to 0.15625
Outputs:
- attended: bfloat16 [16384, 6144], P('seq', 'tp')
- grad_query: bfloat16 [16384, 6144], P('seq', 'tp')
- grad_latents: float32 [32, 64, 1280], P('seq')
- grad_key_weight: float32 [1280, 6144], P('seq', 'tp')
- grad_value_weight: float32 [1280, 6144], P('seq', 'tp')
The draws below stay inside these ranges and needn't reach their ends.
Inputs may be any that keep to these rules, and one draw needn't show every extreme that they name: `token_image`: the value 32 marks a token that attends no image. A token of seq index d attends only the slot d or one of the 4 slots before it, and in every draw some token attends the slot exactly 4 before its own. The tokens that attend one slot form one contiguous run that begins among that slot's own seq index's tokens. A slot is attended by some token exactly when its patch_count is positive. `patch_count`: 0 marks an empty slot; 256 is reached in every draw.
All inputs are finite; a program needn't handle non-finite values.
Results may differ from the reference program's by a relative error of at most 0.03.
Values may be sent and summed in bfloat16 or wider, within the bound.
A program may use at most 64 MiB of HBM per device.

```python
import jax
import jax.numpy as jnp
from jax import lax

H = 48
HD = 128
L = 64
VD = 1280
RH = 8
RHD = 96
P_SIZE = 256
REACH = 4
TOK_DEV = 512
RI = 768
SLOTS = 32
TOKENS = 16384


def layout_draw(key):
    sub_keys = jax.random.split(jax.random.fold_in(key, 4099), 5)
    device_index = jnp.arange(SLOTS, dtype=jnp.int32)
    present = jax.random.randint(sub_keys[0], (SLOTS,), 0, 3) > 0
    forced = jax.random.randint(sub_keys[1], (), 0, SLOTS - REACH)
    quiet = jnp.logical_and(device_index > forced, device_index <= forced + REACH)
    present = jnp.where(device_index == forced, True, jnp.where(quiet, False, present))
    offset = jax.random.randint(sub_keys[2], (SLOTS,), 0, TOK_DEV)
    offset = jnp.where(device_index == 0, jnp.maximum(offset, 1), offset)
    begins = device_index * TOK_DEV + offset
    span_length = jax.random.randint(sub_keys[3], (SLOTS,), 1, (REACH + 1) * TOK_DEV + 1)
    span_length = jnp.where(device_index == forced, (REACH + 1) * TOK_DEV, span_length)
    finish = jnp.minimum(begins + span_length, (device_index + REACH + 1) * TOK_DEV)
    patch_live = jax.random.randint(sub_keys[4], (SLOTS,), 1, P_SIZE + 1)
    patch_live = jnp.where(device_index == forced, P_SIZE, patch_live)
    patch_live = jnp.where(present, patch_live, 0)
    return (present, begins, finish, patch_live)


def draw_token_image(key, part):
    present, begins, finish, patch_live = layout_draw(key)
    device_index = jnp.arange(SLOTS, dtype=jnp.int32)
    marker = jnp.zeros((TOKENS,), jnp.int32).at[begins].max(jnp.where(present, device_index + 1, 0))
    latest = lax.cummax(marker)
    image_ids = latest - 1
    position = jnp.arange(TOKENS, dtype=jnp.int32)
    alive = jnp.logical_and(latest > 0, position < finish[jnp.maximum(image_ids, 0)])
    return jnp.where(alive, image_ids, SLOTS).astype(jnp.int32)


def draw_patch_count(key, part):
    return layout_draw(key)[3].astype(jnp.int32)


def levels(stream_key, shape, shards, smallest, largest):
    loudness = 1.0
    for dim, blocks in shards:
        heights = jax.random.uniform(jax.random.fold_in(jax.random.fold_in(stream_key, 6), dim), (blocks,), jnp.float32, smallest / len(shards), largest / len(shards))
        loudness = loudness * jnp.repeat(jnp.exp(heights), shape[dim] // blocks).reshape((-1,) + (1,) * (len(shape) - 1 - dim))
    return loudness


def noise(key, shape, scale, limit, cuts=(), kind=jnp.bfloat16):
    entries = scale * jax.random.normal(key, shape, jnp.float32)
    if cuts:
        entries = entries * levels(key, shape, cuts, -0.22, 0.18)
    return jnp.clip(entries, -limit, limit).astype(kind)


def setup_inputs(seed: int = 0) -> dict:
    keys = jax.random.split(jax.random.key(seed), 14)
    queries = noise(keys[0], (TOKENS, H * HD), 1.0, 6.0, ((0, 32), (1, 24)))
    cotangent = noise(keys[1], (TOKENS, H * HD), 1.0, 6.0, ((0, 32), (1, 24)))
    gate = jnp.clip(0.2 + 1.3 * jax.random.uniform(keys[2], (H,), jnp.float32) ** levels(keys[2], (H,), ((0, 24),), -0.2, 0.2), 0.2, 1.5)
    token_image = draw_token_image(jax.random.fold_in(keys[13], 71), 0)
    patches = noise(keys[4], (SLOTS, P_SIZE, VD), 1.0, 6.0, ((0, 32),))
    patch_count = draw_patch_count(jax.random.fold_in(keys[13], 71), 0)
    latents = noise(keys[6], (L, VD), 1.0, 6.0)
    latent_queries = noise(keys[7], (L, RI), 1.0, 6.0)
    rs_key = noise(keys[8], (VD, RI), VD ** -0.5, 0.15625)
    rs_value = noise(keys[9], (VD, RI), VD ** -0.5, 0.15625)
    rs_out = noise(keys[10], (RI, VD), RI ** -0.5, 0.21875)
    key_weight = noise(keys[11], (VD, H * HD), VD ** -0.5, 0.15625, ((1, 24),))
    value_weight = noise(keys[12], (VD, H * HD), VD ** -0.5, 0.15625, ((1, 24),))
    return {"queries": queries, "cotangent": cotangent, "gate": gate, "token_image": token_image, "patches": patches, "patch_count": patch_count, "latents": latents, "latent_queries": latent_queries, "rs_key": rs_key, "rs_value": rs_value, "rs_out": rs_out, "key_weight": key_weight, "value_weight": value_weight}


EPS = 1e-05

def norm_rows(matrix):
    matrix = matrix.astype(jnp.float32)
    average = lax.optimization_barrier(jnp.mean(matrix, axis=-1, keepdims=True))
    centered = matrix - average
    variance = lax.optimization_barrier(jnp.mean(centered * centered, axis=-1, keepdims=True))
    return centered * lax.rsqrt(variance + EPS)

def norm_back(matrix, incoming):
    matrix = matrix.astype(jnp.float32)
    average = lax.optimization_barrier(jnp.mean(matrix, axis=-1, keepdims=True))
    centered = matrix - average
    variance = lax.optimization_barrier(jnp.mean(centered * centered, axis=-1, keepdims=True))
    inverse = lax.rsqrt(variance + EPS)
    normed = centered * inverse
    first_mean = lax.optimization_barrier(jnp.mean(incoming, axis=-1, keepdims=True))
    second_mean = lax.optimization_barrier(jnp.mean(incoming * normed, axis=-1, keepdims=True))
    return inverse * (incoming - first_mean - normed * second_mean)

def head_norm(matrix, head_width):
    layout = matrix.shape
    pieces = matrix.reshape(layout[:-1] + (layout[-1] // head_width, head_width))
    return norm_rows(pieces).reshape(layout)

def head_back(matrix, incoming, head_width):
    layout = matrix.shape
    split_layout = layout[:-1] + (layout[-1] // head_width, head_width)
    return norm_back(matrix.reshape(split_layout), incoming.reshape(split_layout)).reshape(layout)

def round_half(matrix):
    return lax.optimization_barrier(matrix.astype(jnp.bfloat16)).astype(jnp.float32)

def resample(patch_rows, live_count, latents, query_hat, rs_key, rs_value, rs_out):
    inputs = jnp.concatenate([norm_rows(patch_rows), norm_rows(latents)], axis=0).astype(jnp.bfloat16)
    key_rows = head_norm(jnp.dot(inputs, rs_key, preferred_element_type=jnp.float32), RHD).astype(jnp.bfloat16)
    value_rows = jnp.dot(inputs, rs_value, preferred_element_type=jnp.float32).astype(jnp.bfloat16)
    row_total = inputs.shape[0]
    query_heads = query_hat.reshape(L, RH, RHD).astype(jnp.float32)
    key_heads = key_rows.reshape(row_total, RH, RHD).astype(jnp.float32)
    value_heads = value_rows.reshape(row_total, RH, RHD).astype(jnp.float32)
    scores = jnp.einsum('lhd,khd->hlk', query_heads, key_heads) / RHD ** 0.5
    position = jnp.arange(row_total, dtype=jnp.int32)
    kept_mask = jnp.logical_or(position < live_count, position >= P_SIZE).astype(jnp.float32)
    weights = jnp.exp(scores) * kept_mask
    probability = round_half(weights / lax.optimization_barrier(jnp.sum(weights, axis=-1, keepdims=True)))
    context = jnp.einsum('hlk,khd->lhd', probability, value_heads)
    context = context.reshape(L, RH * RHD).astype(jnp.bfloat16)
    return latents.astype(jnp.float32) + jnp.dot(context, rs_out, preferred_element_type=jnp.float32)

def cross_latents(resampled, key_weight, value_weight):
    lat_normed = norm_rows(resampled).astype(jnp.bfloat16)
    key_raw = jnp.dot(lat_normed, key_weight, preferred_element_type=jnp.float32)
    key_hat = head_norm(key_raw, HD).astype(jnp.bfloat16)
    value_rows = jnp.dot(lat_normed, value_weight, preferred_element_type=jnp.float32).astype(jnp.bfloat16)
    return (lat_normed, key_raw, key_hat, value_rows)

def reference(queries, cotangent, gate, token_image, patches, patch_count, latents, latent_queries, rs_key, rs_value, rs_out, key_weight, value_weight):
    query_hat = head_norm(latent_queries, RHD).astype(jnp.bfloat16)

    def one_image(element):
        patch_rows, live_count = element
        resampled = resample(patch_rows, live_count, latents, query_hat, rs_key, rs_value, rs_out)
        lat_normed, key_raw, key_hat, value_rows = cross_latents(resampled, key_weight, value_weight)
        return (resampled, lat_normed, key_raw, key_hat, value_rows)
    resampled, lat_normed, key_raw, key_hat, value_rows = lax.map(one_image, (patches, patch_count))
    cross_width = H * HD
    empty_image = jnp.zeros((1, L, cross_width), jnp.bfloat16)
    key_table = jnp.concatenate([key_hat, empty_image], axis=0)
    value_table = jnp.concatenate([value_rows, empty_image], axis=0)
    text_hat = head_norm(queries, HD).astype(jnp.bfloat16)
    gate_cols = jnp.repeat(jnp.tanh(gate.astype(jnp.float32)), HD)
    block_rows = 64
    block_count = TOKENS // block_rows

    def text_block(running, element):
        grad_key, grad_value = running
        query_rows, incoming, image_ids = element
        has_image = (image_ids < SLOTS).astype(jnp.float32)[:, None]
        key_heads = key_table[image_ids].reshape(block_rows, L, H, HD).astype(jnp.float32)
        value_heads = value_table[image_ids].reshape(block_rows, L, H, HD).astype(jnp.float32)
        query_heads = query_rows.reshape(block_rows, H, HD).astype(jnp.float32)
        scores = jnp.einsum('bhd,blhd->bhl', query_heads, key_heads) / HD ** 0.5
        weights = jnp.exp(scores)
        probability = weights / lax.optimization_barrier(jnp.sum(weights, axis=-1, keepdims=True))
        rounded = round_half(probability)
        context = jnp.einsum('bhl,blhd->bhd', rounded, value_heads).reshape(block_rows, cross_width)
        output = (gate_cols * context * has_image).astype(jnp.bfloat16)
        grad_heads = round_half(gate_cols * incoming.astype(jnp.float32) * has_image).reshape(block_rows, H, HD)
        grad_probs = jnp.einsum('bhd,blhd->bhl', grad_heads, value_heads)
        grad_scores = probability * (grad_probs - lax.optimization_barrier(jnp.sum(probability * grad_probs, axis=-1, keepdims=True)))
        score_rounded = round_half(grad_scores)
        grad_qhat = jnp.einsum('bhl,blhd->bhd', score_rounded, key_heads).reshape(block_rows, cross_width) / HD ** 0.5
        key_terms = jnp.einsum('bhl,bhd->blhd', score_rounded, query_heads).reshape(block_rows, L, cross_width) / HD ** 0.5
        value_terms = jnp.einsum('bhl,bhd->blhd', rounded, grad_heads).reshape(block_rows, L, cross_width)
        grad_key = grad_key.at[image_ids].add(key_terms)
        grad_value = grad_value.at[image_ids].add(value_terms)
        return ((grad_key, grad_value), (output, grad_qhat))
    start_sums = (jnp.zeros((SLOTS + 1, L, cross_width), jnp.float32), jnp.zeros((SLOTS + 1, L, cross_width), jnp.float32))
    block_inputs = (text_hat.reshape(block_count, block_rows, cross_width), cotangent.reshape(block_count, block_rows, cross_width), token_image.reshape(block_count, block_rows))
    (grad_key, grad_value), (output, grad_qhat) = lax.scan(text_block, start_sums, block_inputs)
    attended = output.reshape(TOKENS, cross_width)
    grad_query = head_back(queries, grad_qhat.reshape(TOKENS, cross_width), HD).astype(jnp.bfloat16)
    grad_key_raw = head_back(key_raw, grad_key[:SLOTS], HD)
    key_low = grad_key_raw.astype(jnp.bfloat16).reshape(SLOTS * L, cross_width)
    value_low = grad_value[:SLOTS].astype(jnp.bfloat16).reshape(SLOTS * L, cross_width)
    grad_normed = jnp.dot(key_low, key_weight.T, preferred_element_type=jnp.float32) + jnp.dot(value_low, value_weight.T, preferred_element_type=jnp.float32)
    grad_latents = norm_back(resampled, grad_normed.reshape(SLOTS, L, VD))
    flat_normed = lat_normed.reshape(SLOTS * L, VD)
    grad_key_weight = jnp.dot(flat_normed.T, key_low, preferred_element_type=jnp.float32)
    grad_value_weight = jnp.dot(flat_normed.T, value_low, preferred_element_type=jnp.float32)
    return (attended, grad_query, grad_latents, grad_key_weight, grad_value_weight)
```

```python
import functools

import jax
import jax.numpy as jnp
from jax import lax
from jax.experimental import pallas as pl
from jax.experimental.pallas import tpu as pltpu
from jax.sharding import PartitionSpec as P

HD = 128
RHD = 96
REACH = 4
EPS = 1e-05
XS, YS, CS = 4, 4, 2
MESH = pl.DeviceIdType.MESH
F32 = jnp.float32
BF16 = jnp.bfloat16
NT = (((1,), (1,)), ((), ()))
TN = (((0,), (0,)), ((), ()))


def mm(a, b, dims=(((1,), (0,)), ((), ()))):
    return lax.dot_general(a, b, dims, preferred_element_type=F32)


def norm_stats(matrix):
    average = jnp.mean(matrix, axis=-1, keepdims=True)
    centered = matrix - average
    variance = jnp.mean(centered * centered, axis=-1, keepdims=True)
    inverse = lax.rsqrt(variance + EPS)
    return centered * inverse, inverse


def norm_rows(matrix):
    return norm_stats(matrix.astype(F32))[0]


def norm_back(matrix, incoming):
    normed, inverse = norm_stats(matrix)
    first_mean = jnp.mean(incoming, axis=-1, keepdims=True)
    second_mean = jnp.mean(incoming * normed, axis=-1, keepdims=True)
    return inverse * (incoming - first_mean - normed * second_mean)


def resample_kernel(
    count_ref,
    patches_ref,
    latents_ref,
    lq_ref,
    rs_key_ref,
    rs_value_ref,
    rs_out_ref,
    kw_ref,
    vw_ref,
    kv_ref,
    key_raw_ref,
    resampled_ref,
    lat_ref,
    inputs,
    keys,
    values,
):
    n_patch = patches_ref.shape[0]
    n_lat = latents_ref.shape[0]
    rows = n_patch + n_lat
    for r in range(0, n_patch, 64):
        inputs[r : r + 64, :] = norm_rows(patches_ref[r : r + 64, :]).astype(BF16)
    inputs[n_patch:, :] = norm_rows(latents_ref[...]).astype(BF16)
    keys[...] = mm(inputs[...], rs_key_ref[...])
    values[...] = mm(inputs[...], rs_value_ref[...])
    position = lax.broadcasted_iota(jnp.int32, (n_lat, rows), 1)
    kept = jnp.logical_or(position < count_ref[0], position >= n_patch)
    total = latents_ref[...].astype(F32)
    queries = lq_ref[...].astype(F32)
    for h in range(lq_ref.shape[1] // RHD):
        cols = slice(h * RHD, (h + 1) * RHD)
        key_h = norm_rows(keys[:, cols]).astype(BF16)
        query_h = norm_rows(queries[:, cols]).astype(BF16)
        scores = mm(query_h, key_h, NT) / RHD**0.5
        weights = jnp.where(kept, jnp.exp(scores), 0.0)
        prob = (weights / jnp.sum(weights, axis=-1, keepdims=True)).astype(BF16)
        context = mm(prob, values[:, cols].astype(BF16)).astype(BF16)
        total = total + mm(context, rs_out_ref[cols, :])
    resampled_ref[...] = total
    lat = norm_rows(total).astype(BF16)
    lat_ref[...] = lat
    key_raw = mm(lat, kw_ref[...])
    key_raw_ref[...] = key_raw
    width = kw_ref.shape[1]
    for h in range(width // HD):
        cols = slice(h * HD, (h + 1) * HD)
        kv_ref[:, cols] = norm_rows(key_raw[:, cols]).astype(BF16)
    kv_ref[:, width:] = mm(lat, vw_ref[...]).astype(BF16)


def window_kernel(n_seq, kv_ref, window_ref, own_sem, send_sem, recv_sem):
    s = lax.axis_index("seq")
    barrier = pltpu.get_barrier_semaphore()
    for d in range(1, REACH + 1):
        for other in (lax.rem(s + d, n_seq), lax.rem(s + n_seq - d, n_seq)):
            pl.semaphore_signal(barrier, inc=1, device_id={"seq": other}, device_id_type=MESH)
    pl.semaphore_wait(barrier, 2 * REACH)
    copies = []
    for d in range(REACH, 0, -1):
        copy = pltpu.make_async_remote_copy(
            src_ref=kv_ref,
            dst_ref=window_ref.at[REACH - d],
            send_sem=send_sem.at[d - 1],
            recv_sem=recv_sem.at[d - 1],
            device_id={"seq": lax.rem(s + d, n_seq)},
            device_id_type=MESH,
        )
        copy.start()
        copies.append(copy)
    own = pltpu.make_async_copy(kv_ref, window_ref.at[REACH], own_sem)
    own.start()
    own.wait()
    for copy in copies:
        copy.wait()


def text_kernel(
    n_slots,
    seq_ref,
    q_ref,
    cot_ref,
    gate_ref,
    image_ref,
    window_ref,
    att_ref,
    gq_ref,
    away_ref,
    home_ref,
    acc,
):
    step = pl.program_id(0)
    width = q_ref.shape[1]
    slots, n_lat, _ = window_ref.shape
    span = slots * n_lat
    tokens = q_ref.shape[0]
    image = image_ref[...].reshape(1, tokens)
    slot_of = lax.broadcasted_iota(jnp.int32, (span, tokens), 0) // n_lat + (seq_ref[0] - REACH)
    match = slot_of == image
    no_image = (image >= n_slots).astype(F32)
    gates = jnp.tanh(gate_ref[...])
    scale = HD**0.5
    for h in range(width // HD):
        cols = slice(h * HD, (h + 1) * HD)
        vcols = slice(width + h * HD, width + (h + 1) * HD)
        key_w = window_ref[:, :, cols].reshape(span, HD)
        value_w = window_ref[:, :, vcols].reshape(span, HD)
        normed, inverse = norm_stats(q_ref[:, cols].astype(F32))
        text = normed.astype(BF16)
        gate_h = gates[:, h : h + 1]
        grad_ctx = (gate_h * cot_ref[:, cols].astype(F32)).astype(BF16)
        weights = jnp.where(match, jnp.exp(mm(key_w, text, NT) / scale), 0.0)
        denominator = jnp.sum(weights, axis=0, keepdims=True) + no_image
        prob = weights / denominator
        low = prob.astype(BF16)
        att_ref[:, cols] = (gate_h * mm(low, value_w, TN)).astype(BF16)
        grad_prob = mm(value_w, grad_ctx, NT)
        inner = jnp.sum(prob * grad_prob, axis=0, keepdims=True)
        grad_score = (prob * (grad_prob - inner)).astype(BF16)
        grad_hat = mm(grad_score, key_w, TN) / scale
        first = jnp.mean(grad_hat, axis=-1, keepdims=True)
        second = jnp.mean(grad_hat * normed, axis=-1, keepdims=True)
        gq_ref[:, cols] = (inverse * (grad_hat - first - normed * second)).astype(BF16)
        key_term = mm(grad_score, text) / scale
        value_term = mm(low, grad_ctx)

        @pl.when(step == 0)
        def _():
            acc[:, cols] = key_term
            acc[:, vcols] = value_term

        @pl.when(step > 0)
        def _():
            acc[:, cols] += key_term
            acc[:, vcols] += value_term

    @pl.when(step == pl.num_programs(0) - 1)
    def _():
        away_ref[...] = acc[: REACH * n_lat, :].astype(BF16).reshape(REACH, n_lat, 2 * width)
        home_ref[...] = acc[REACH * n_lat :, :]


def gather_kernel(
    n_seq,
    n_tp,
    n_red,
    away_ref,
    home_ref,
    key_raw_ref,
    lat_ref,
    resampled_ref,
    kw_ref,
    vw_ref,
    glat_ref,
    gk_ref,
    gv_ref,
    back,
    parts,
    parts_in,
    result,
    gathered,
    prod,
    r1,
    a1,
    r2,
    r3,
    r4,
    a2,
    u2,
    u3,
    u4,
    back_send,
    back_recv,
    red_send,
    red_recv,
    all_send,
    all_recv,
    sems,
    recvs,
):
    s = lax.axis_index("seq")
    t = lax.axis_index("tp")
    width = kw_ref.shape[1]
    n_lat, n_col = lat_ref.shape
    half = n_lat // 2
    blocks = n_col // HD
    core = lax.rem(s, CS)
    chip = lax.div(s, CS)
    y = lax.rem(chip, YS)
    x = lax.div(chip, YS)

    def seq_of(xx, yy, cc):
        return (xx * YS + yy) * CS + cc

    partner = seq_of(x, y, 1 - core)
    x_up, x_dn, x_far = lax.rem(x + 1, XS), lax.rem(x + XS - 1, XS), lax.rem(x + 2, XS)
    y_up, y_dn, y_far = lax.rem(y + 1, YS), lax.rem(y + YS - 1, YS), lax.rem(y + 2, YS)
    to_xu, to_xd = seq_of(x_up, y, core), seq_of(x_dn, y, core)
    to_yu, to_yd = seq_of(x, y_up, core), seq_of(x, y_dn, core)

    barrier = pltpu.get_barrier_semaphore()
    friends = [partner, to_xu, to_xd, to_yu, to_yd]
    for d in range(1, REACH + 1):
        friends += [lax.rem(s + d, n_seq), lax.rem(s + n_seq - d, n_seq)]
    for other in friends:
        pl.semaphore_signal(barrier, inc=1, device_id={"seq": other}, device_id_type=MESH)
    for i in range(1, n_tp):
        pl.semaphore_signal(
            barrier, inc=1, device_id={"tp": lax.rem(t + i, n_tp)}, device_id_type=MESH
        )
    pl.semaphore_wait(barrier, len(friends) + n_tp - 1)

    def send(src, dst, index, to):
        copy = pltpu.make_async_remote_copy(
            src_ref=src,
            dst_ref=dst,
            send_sem=sems.at[index],
            recv_sem=recvs.at[index],
            device_id={"seq": to},
            device_id_type=MESH,
        )
        copy.start()
        return copy

    copies = []
    for d in range(REACH, 0, -1):
        copy = pltpu.make_async_remote_copy(
            src_ref=away_ref.at[REACH - d],
            dst_ref=back.at[d - 1],
            send_sem=back_send.at[d - 1],
            recv_sem=back_recv.at[d - 1],
            device_id={"seq": lax.rem(s + n_seq - d, n_seq)},
            device_id_type=MESH,
        )
        copy.start()
        copies.append(copy)
    for copy in copies:
        copy.wait()
    reduced = home_ref[...]
    for d in range(REACH):
        reduced = reduced + back[d].astype(F32)
    lows = []
    for h in range(width // HD):
        cols = slice(h * HD, (h + 1) * HD)
        lows.append(norm_back(key_raw_ref[:, cols], reduced[:, cols]).astype(BF16))
    key_low = jnp.concatenate(lows, axis=1)
    value_low = reduced[:, width:].astype(BF16)

    for j in range(blocks):
        rows = slice(j * HD, (j + 1) * HD)
        part = mm(key_low, kw_ref[rows, :], NT) + mm(value_low, vw_ref[rows, :], NT)
        parts[j] = part[:half].astype(BF16)
        parts[blocks + j] = part[half:].astype(BF16)

    def red_copy(i):
        to = lax.rem(t + i, n_tp)
        return to, pltpu.make_async_remote_copy(
            src_ref=parts.at[lax.min(to, n_red - 1)],
            dst_ref=parts_in.at[i - 1],
            send_sem=red_send.at[i - 1],
            recv_sem=red_recv.at[i - 1],
            device_id={"tp": to},
            device_id_type=MESH,
        )

    for i in range(1, n_tp):
        to, copy = red_copy(i)

        @pl.when(to < n_red)
        def _():
            copy.start()

    low = jnp.concatenate([key_low, value_low], axis=1)
    n_out = n_col // n_seq
    chips_per = n_seq // 4
    piece = chips_per * CS * n_out
    for j in range(n_col // piece):
        full = mm(lat_ref[:, j * piece : (j + 1) * piece], low, TN)
        for p in range(chips_per):
            for c in range(CS):
                start = (p * CS + c) * n_out
                prod[c, j * chips_per + p] = full[start : start + n_out].astype(BF16)
    core_copy = send(prod.at[1 - core], r1, 0, partner)

    def all_copy(i):
        to = lax.rem(t + i, n_tp)
        slot = lax.min(t, n_red - 1)
        return pltpu.make_async_remote_copy(
            src_ref=result,
            dst_ref=gathered.at[slot],
            send_sem=all_send.at[i - 1],
            recv_sem=all_recv.at[slot],
            device_id={"tp": to},
            device_id_type=MESH,
        )

    def from_copy(r):
        return pltpu.make_async_remote_copy(
            src_ref=result,
            dst_ref=gathered.at[r],
            send_sem=all_send.at[0],
            recv_sem=all_recv.at[r],
            device_id={"tp": lax.rem(t + 1, n_tp)},
            device_id_type=MESH,
        )

    @pl.when(t < n_red)
    def _():
        for i in range(1, n_tp):
            red_copy(i)[1].wait_recv()
        total = parts[lax.min(t, n_red - 1)].astype(F32)
        for i in range(n_tp - 1):
            total = total + parts_in[i].astype(F32)
        result[...] = total.astype(BF16)
        for i in range(1, n_tp):
            all_copy(i).start()

    core_copy.wait()
    for xx in range(XS):
        rows = slice(xx * YS, (xx + 1) * YS)
        a1[xx] = (prod[core, rows].astype(F32) + r1[rows].astype(F32)).astype(BF16)
    hy = YS // 2
    c1 = send(a1.at[x_far, :hy], r2.at[0], 1, to_xu)
    c2 = send(a1.at[x_far, hy:], r2.at[1], 2, to_xd)
    c3 = send(a1.at[x_up, hy:], r3.at[hy:], 3, to_xu)
    c4 = send(a1.at[x_dn, :hy], r4.at[:hy], 4, to_xd)
    c1.wait()
    a1[x_up, :hy] = (a1[x_up, :hy].astype(F32) + r2[0].astype(F32)).astype(BF16)
    c5 = send(a1.at[x_up, :hy], r3.at[:hy], 5, to_xu)
    c2.wait()
    a1[x_dn, hy:] = (a1[x_dn, hy:].astype(F32) + r2[1].astype(F32)).astype(BF16)
    c6 = send(a1.at[x_dn, hy:], r4.at[hy:], 6, to_xd)
    c3.wait()
    c4.wait()
    c5.wait()
    c6.wait()
    for yy in range(YS):
        value = a1[x, yy].astype(F32) + r3[yy].astype(F32) + r4[yy].astype(F32)
        a2[yy, 0] = value[:, :width].astype(BF16)
        a2[yy, 1] = value[:, width:].astype(BF16)
    d1 = send(a2.at[y_far, 0], u2.at[0], 7, to_yu)
    d2 = send(a2.at[y_far, 1], u2.at[1], 8, to_yd)
    d3 = send(a2.at[y_up, 1], u3.at[1], 9, to_yu)
    d4 = send(a2.at[y_dn, 0], u4.at[0], 10, to_yd)
    d1.wait()
    a2[y_up, 0] = (a2[y_up, 0].astype(F32) + u2[0].astype(F32)).astype(BF16)
    d5 = send(a2.at[y_up, 0], u3.at[0], 11, to_yu)
    d2.wait()
    a2[y_dn, 1] = (a2[y_dn, 1].astype(F32) + u2[1].astype(F32)).astype(BF16)
    d6 = send(a2.at[y_dn, 1], u4.at[1], 12, to_yd)
    d3.wait()
    d4.wait()
    d5.wait()
    d6.wait()
    gk_ref[...] = a2[y, 0].astype(F32) + u3[0].astype(F32) + u4[0].astype(F32)
    gv_ref[...] = a2[y, 1].astype(F32) + u3[1].astype(F32) + u4[1].astype(F32)

    for r in range(n_red):

        @pl.when(t != r)
        def _():
            from_copy(r).wait_recv()

    for i in range(1, n_tp):
        to, copy = red_copy(i)

        @pl.when(to < n_red)
        def _():
            copy.wait_send()

    @pl.when(t < n_red)
    def _():
        for i in range(1, n_tp):
            all_copy(i).wait_send()
        gathered[lax.min(t, n_red - 1)] = result[...]

    for k in range(2):
        rows = slice(k * half, (k + 1) * half)
        grad = jnp.concatenate(
            [gathered[k * blocks + j].astype(F32) for j in range(blocks)], axis=1
        )
        glat_ref[rows, :] = norm_back(resampled_ref[rows, :], grad)


def on_device(
    queries,
    cotangent,
    gate,
    token_image,
    patches,
    patch_count,
    latents,
    latent_queries,
    rs_key,
    rs_value,
    rs_out,
    key_weight,
    value_weight,
):
    n_seq = lax.axis_size("seq")
    n_tp = lax.axis_size("tp")
    width = key_weight.shape[1]
    tokens = queries.shape[0]
    n_lat, n_col = latents.shape
    n_patch = patches.shape[1]
    inner = latent_queries.shape[1]
    rows = n_patch + n_lat
    vmem = pl.BlockSpec(memory_space=pltpu.VMEM)
    smem = pl.BlockSpec(memory_space=pltpu.SMEM)
    kv, key_raw, resampled, lat = pl.pallas_call(
        resample_kernel,
        name="resample",
        out_shape=(
            jax.ShapeDtypeStruct((n_lat, 2 * width), BF16),
            jax.ShapeDtypeStruct((n_lat, width), F32),
            jax.ShapeDtypeStruct((n_lat, n_col), F32),
            jax.ShapeDtypeStruct((n_lat, n_col), BF16),
        ),
        in_specs=[smem] + [vmem] * 8,
        out_specs=(vmem,) * 4,
        scratch_shapes=[
            pltpu.VMEM((rows, n_col), BF16),
            pltpu.VMEM((rows, inner), F32),
            pltpu.VMEM((rows, inner), F32),
        ],
    )(
        patch_count,
        patches[0],
        latents,
        latent_queries,
        rs_key,
        rs_value,
        rs_out,
        key_weight,
        value_weight,
    )
    window = pl.pallas_call(
        functools.partial(window_kernel, n_seq),
        name="window",
        out_shape=jax.ShapeDtypeStruct((REACH + 1, n_lat, 2 * width), BF16),
        in_specs=[vmem],
        out_specs=vmem,
        scratch_shapes=[
            pltpu.SemaphoreType.DMA(()),
            pltpu.SemaphoreType.DMA((REACH,)),
            pltpu.SemaphoreType.DMA((REACH,)),
        ],
        compiler_params=pltpu.CompilerParams(collective_id=0, has_side_effects=True),
    )(kv)
    block = 256
    span = (REACH + 1) * n_lat
    seq_rank = lax.axis_index("seq").astype(jnp.int32).reshape(1)
    token_spec = pl.BlockSpec((block, width), lambda i: (i, 0))
    attended, grad_query, away, home = pl.pallas_call(
        functools.partial(text_kernel, n_seq),
        name="text",
        grid=(tokens // block,),
        out_shape=(
            jax.ShapeDtypeStruct((tokens, width), BF16),
            jax.ShapeDtypeStruct((tokens, width), BF16),
            jax.ShapeDtypeStruct((REACH, n_lat, 2 * width), BF16),
            jax.ShapeDtypeStruct((n_lat, 2 * width), F32),
        ),
        in_specs=[
            smem,
            token_spec,
            token_spec,
            pl.BlockSpec((1, width // HD), lambda i: (0, 0)),
            pl.BlockSpec((1, 1, block), lambda i: (i, 0, 0)),
            pl.BlockSpec((REACH + 1, n_lat, 2 * width), lambda i: (0, 0, 0)),
        ],
        out_specs=(
            token_spec,
            token_spec,
            pl.BlockSpec((REACH, n_lat, 2 * width), lambda i: (0, 0, 0)),
            pl.BlockSpec((n_lat, 2 * width), lambda i: (0, 0)),
        ),
        scratch_shapes=[pltpu.VMEM((span, 2 * width), F32)],
    )(
        seq_rank,
        queries,
        cotangent,
        gate.reshape(1, width // HD),
        token_image.reshape(tokens // block, 1, block),
        window,
    )
    n_red = 2 * (n_col // HD)
    n_out = n_col // n_seq
    half = n_lat // 2
    dma = pltpu.SemaphoreType.DMA
    grad_latents, grad_key_weight, grad_value_weight = pl.pallas_call(
        functools.partial(gather_kernel, n_seq, n_tp, n_red),
        name="gather",
        out_shape=(
            jax.ShapeDtypeStruct((n_lat, n_col), F32),
            jax.ShapeDtypeStruct((n_out, width), F32),
            jax.ShapeDtypeStruct((n_out, width), F32),
        ),
        in_specs=[vmem] * 7,
        out_specs=(vmem,) * 3,
        scratch_shapes=[
            pltpu.VMEM((REACH, n_lat, 2 * width), BF16),
            pltpu.VMEM((n_red, half, HD), BF16),
            pltpu.VMEM((n_tp - 1, half, HD), BF16),
            pltpu.VMEM((half, HD), BF16),
            pltpu.VMEM((n_red, half, HD), BF16),
            pltpu.VMEM((CS, XS * YS, n_out, 2 * width), BF16),
            pltpu.VMEM((XS * YS, n_out, 2 * width), BF16),
            pltpu.VMEM((XS, YS, n_out, 2 * width), BF16),
            pltpu.VMEM((2, YS // 2, n_out, 2 * width), BF16),
            pltpu.VMEM((YS, n_out, 2 * width), BF16),
            pltpu.VMEM((YS, n_out, 2 * width), BF16),
            pltpu.VMEM((YS, 2, n_out, width), BF16),
            pltpu.VMEM((2, n_out, width), BF16),
            pltpu.VMEM((2, n_out, width), BF16),
            pltpu.VMEM((2, n_out, width), BF16),
            dma((REACH,)),
            dma((REACH,)),
            dma((n_tp - 1,)),
            dma((n_tp - 1,)),
            dma((n_tp - 1,)),
            dma((n_red,)),
            dma((13,)),
            dma((13,)),
        ],
        compiler_params=pltpu.CompilerParams(collective_id=1, has_side_effects=True),
    )(away, home, key_raw, lat, resampled, key_weight, value_weight)
    return (attended, grad_query, grad_latents[None], grad_key_weight, grad_value_weight)


def solution(mesh):
    placed = (
        P("seq", "tp"),
        P("seq", "tp"),
        P("tp"),
        P("seq"),
        P("seq", None, None),
        P("seq"),
        P(),
        P(),
        P(),
        P(),
        P(),
        P(None, "tp"),
        P(None, "tp"),
    )
    return jax.shard_map(
        on_device,
        mesh=mesh,
        in_specs=placed,
        out_specs=(
            P("seq", "tp"),
            P("seq", "tp"),
            P("seq", None, None),
            P("seq", "tp"),
            P("seq", "tp"),
        ),
        check_vma=False,
    )
```

```python
import functools

import jax
import jax.numpy as jnp
from jax import lax
from jax.experimental import pallas as pl
from jax.experimental.pallas import tpu as pltpu
from jax.sharding import PartitionSpec as P

HD = 128
RHD = 96
REACH = 4
EPS = 1e-05
XS, YS, CS = 4, 4, 2
MESH = pl.DeviceIdType.MESH
F32 = jnp.float32
BF16 = jnp.bfloat16
NT = (((1,), (1,)), ((), ()))
TN = (((0,), (0,)), ((), ()))


def mm(a, b, dims=(((1,), (0,)), ((), ()))):
    return lax.dot_general(a, b, dims, preferred_element_type=F32)


def norm_stats(matrix):
    average = jnp.mean(matrix, axis=-1, keepdims=True)
    centered = matrix - average
    variance = jnp.mean(centered * centered, axis=-1, keepdims=True)
    inverse = lax.rsqrt(variance + EPS)
    return centered * inverse, inverse


def norm_rows(matrix):
    return norm_stats(matrix.astype(F32))[0]


def norm_back(matrix, incoming):
    normed, inverse = norm_stats(matrix)
    first_mean = jnp.mean(incoming, axis=-1, keepdims=True)
    second_mean = jnp.mean(incoming * normed, axis=-1, keepdims=True)
    return inverse * (incoming - first_mean - normed * second_mean)


def whole_kernel(
    n_seq,
    n_tp,
    n_red,
    count_ref,
    latents_ref,
    lq_ref,
    gate_ref,
    image_ref,
    patches_hbm,
    rs_key_hbm,
    rs_value_hbm,
    rs_out_hbm,
    kw_hbm,
    vw_hbm,
    q_hbm,
    cot_hbm,
    att_ref,
    gq_ref,
    resampled_ref,
    gathered,
    wsum_ref,
    patches_ref,
    rs_key_ref,
    rs_value_ref,
    rs_out_ref,
    kw_ref,
    vw_ref,
    q_ref,
    cot_ref,
    inputs,
    keys,
    values,
    lat_ref,
    key_raw_ref,
    window,
    text,
    grad_ctx,
    probs,
    gscores,
    terms,
    terms_low,
    back_e,
    back_c,
    back_d,
    back_b,
    back_a,
    reduced_ref,
    parts,
    parts_in,
    result,
    prod,
    r1,
    a1,
    r2,
    r3,
    r4,
    a2,
    u2,
    u3,
    u4,
    load_sem,
    win_send,
    win_recv,
    back_send,
    back_recv,
    red_send,
    red_recv,
    all_send,
    all_recv,
    sems,
    recvs,
):
    s = lax.axis_index("seq")
    t = lax.axis_index("tp")
    width = kw_ref.shape[1]
    n_lat, n_col = lat_ref.shape
    half = n_lat // 2
    blocks = n_col // HD
    tokens = q_ref.shape[0]
    core = lax.rem(s, CS)
    chip = lax.div(s, CS)
    y = lax.rem(chip, YS)
    x = lax.div(chip, YS)

    def seq_of(xx, yy, cc):
        return (xx * YS + yy) * CS + cc

    partner = seq_of(x, y, 1 - core)
    ahead, behind = lax.rem(s + CS, n_seq), lax.rem(s + n_seq - CS, n_seq)
    x_up, x_dn, x_far = lax.rem(x + 1, XS), lax.rem(x + XS - 1, XS), lax.rem(x + 2, XS)
    y_up, y_dn, y_far = lax.rem(y + 1, YS), lax.rem(y + YS - 1, YS), lax.rem(y + 2, YS)
    to_xu, to_xd = seq_of(x_up, y, core), seq_of(x_dn, y, core)
    to_yu, to_yd = seq_of(x, y_up, core), seq_of(x, y_dn, core)

    loads = []
    for i, (src, dst) in enumerate(
        (
            (patches_hbm, patches_ref),
            (rs_key_hbm, rs_key_ref),
            (rs_value_hbm, rs_value_ref),
            (rs_out_hbm, rs_out_ref),
            (kw_hbm, kw_ref),
            (vw_hbm, vw_ref),
            (q_hbm, q_ref),
            (cot_hbm, cot_ref),
        )
    ):
        load = pltpu.make_async_copy(src, dst, load_sem.at[i])
        load.start()
        loads.append(load)

    barrier = pltpu.get_barrier_semaphore()
    friends = [partner, ahead, behind, to_xu, to_xd, to_yu, to_yd]
    for other in friends:
        pl.semaphore_signal(barrier, inc=1, device_id={"seq": other}, device_id_type=MESH)
    for i in range(1, n_tp):
        pl.semaphore_signal(
            barrier, inc=1, device_id={"tp": lax.rem(t + i, n_tp)}, device_id_type=MESH
        )

    n_patch = patches_ref.shape[0]
    rows = n_patch + n_lat
    inputs[n_patch:, :] = norm_rows(latents_ref[...]).astype(BF16)
    loads[0].wait()
    for r in range(0, n_patch, 64):
        inputs[r : r + 64, :] = norm_rows(patches_ref[r : r + 64, :]).astype(BF16)
    loads[1].wait()
    keys[...] = mm(inputs[...], rs_key_ref[...])
    loads[2].wait()
    values[...] = mm(inputs[...], rs_value_ref[...])
    loads[3].wait()
    position = lax.broadcasted_iota(jnp.int32, (n_lat, rows), 1)
    kept = jnp.logical_or(position < count_ref[0], position >= n_patch)
    total = latents_ref[...].astype(F32)
    queries = lq_ref[...].astype(F32)
    for h in range(lq_ref.shape[1] // RHD):
        cols = slice(h * RHD, (h + 1) * RHD)
        key_h = norm_rows(keys[:, cols]).astype(BF16)
        query_h = norm_rows(queries[:, cols]).astype(BF16)
        scores = mm(query_h, key_h, NT) / RHD**0.5
        weights = jnp.where(kept, jnp.exp(scores), 0.0)
        prob = (weights / jnp.sum(weights, axis=-1, keepdims=True)).astype(BF16)
        context = mm(prob, values[:, cols].astype(BF16)).astype(BF16)
        total = total + mm(context, rs_out_ref[cols, :])
    resampled_ref[...] = total
    lat = norm_rows(total).astype(BF16)
    lat_ref[...] = lat
    loads[4].wait()
    loads[5].wait()
    key_raw = mm(lat, kw_ref[...])
    key_raw_ref[...] = key_raw
    for h in range(width // HD):
        cols = slice(h * HD, (h + 1) * HD)
        window[REACH, :, cols] = norm_rows(key_raw[:, cols]).astype(BF16)
    window[REACH, :, width:] = mm(lat, vw_ref[...]).astype(BF16)

    pl.semaphore_wait(barrier, len(friends) + n_tp - 1)

    def remote(src, dst, send_sem, recv_sem, to):
        return pltpu.make_async_remote_copy(
            src_ref=src,
            dst_ref=dst,
            send_sem=send_sem,
            recv_sem=recv_sem,
            device_id={"seq": to},
            device_id_type=MESH,
        )

    def pass_on(k_from, k_to, index, to):
        return remote(
            window.at[k_from], window.at[k_to], win_send.at[index], win_recv.at[k_to], to
        )

    pass_a = pass_on(4, 2, 0, ahead)
    pass_b = pass_on(4, 3, 1, partner)
    pass_c = pass_on(2, 0, 2, ahead)
    pass_d0 = pass_on(2, 1, 3, partner)
    pass_d1 = pass_on(2, 3, 3, partner)
    pass_e = pass_on(0, 1, 4, partner)
    pass_a.start()

    @pl.when(core == 0)
    def _():
        pass_b.start()

    gates = jnp.tanh(gate_ref[...])
    scale = HD**0.5
    loads[6].wait()
    loads[7].wait()
    heads = []
    for h in range(width // HD):
        cols = slice(h * HD, (h + 1) * HD)
        vcols = slice(width + h * HD, width + (h + 1) * HD)
        heads.append((h, cols, vcols))
        text[:, cols] = norm_rows(q_ref[:, cols]).astype(BF16)
        grad_ctx[:, cols] = (gates[:, h : h + 1] * cot_ref[:, cols].astype(F32)).astype(BF16)
    image = image_ref[...]

    def attend(k):
        match = image == s - REACH + k
        other = jnp.where(match, 0.0, 1.0)
        lat_rows = slice(k * n_lat, (k + 1) * n_lat)
        for h, cols, vcols in heads:
            scores = mm(window[k, :, cols], text[:, cols], NT) / scale
            weights = jnp.where(match, jnp.exp(scores), 0.0)
            prob = weights / (jnp.sum(weights, axis=0, keepdims=True) + other)
            low = prob.astype(BF16)
            grad_prob = mm(window[k, :, vcols], grad_ctx[:, cols], NT)
            inner = jnp.sum(prob * grad_prob, axis=0, keepdims=True)
            grad_score = (prob * (grad_prob - inner)).astype(BF16)
            probs[h, lat_rows, :] = low
            gscores[h, lat_rows, :] = grad_score
            terms[k, :, cols] = mm(grad_score, text[:, cols]) / scale
            terms[k, :, vcols] = mm(low, grad_ctx[:, cols])

    attend(4)
    pass_a.wait_recv()
    pass_c.start()

    @pl.when(core == 0)
    def _():
        pass_d0.start()

    @pl.when(core == 1)
    def _():
        pass_d1.start()

    attend(2)
    pass_on(4, 3, 1, partner).wait_recv()
    attend(3)
    terms_low[3] = terms[3].astype(BF16)
    pass_c.wait_recv()

    @pl.when(core == 1)
    def _():
        pass_e.start()

    attend(0)
    pass_e.wait_recv()
    attend(1)
    terms_low[1] = terms[1].astype(BF16)

    give_e = remote(terms_low.at[1], back_e, back_send.at[0], back_recv.at[0], partner)
    give_c = remote(terms_low.at[0], back_c, back_send.at[1], back_recv.at[1], behind)
    give_d = remote(
        terms_low.at[3 - 2 * core], back_d, back_send.at[2], back_recv.at[2], partner
    )
    give_b = remote(terms_low.at[3], back_b, back_send.at[3], back_recv.at[3], partner)
    give_a = remote(terms_low.at[2], back_a, back_send.at[4], back_recv.at[4], behind)

    @pl.when(core == 0)
    def _():
        give_e.start()
        terms_low[0] = terms[0].astype(BF16)

    give_d.start()

    @pl.when(core == 1)
    def _():
        give_e.wait_recv()
        terms_low[0] = (terms[0] + back_e[...].astype(F32)).astype(BF16)

    give_c.start()

    @pl.when(core == 1)
    def _():
        give_b.start()

    give_d.wait_recv()
    give_c.wait_recv()
    terms_low[2] = (terms[2] + back_d[...].astype(F32) + back_c[...].astype(F32)).astype(BF16)
    give_a.start()
    reduced_ref[...] = terms[REACH]

    @pl.when(core == 0)
    def _():
        give_b.wait_recv()
        reduced_ref[...] += back_b[...].astype(F32)

    give_a.wait_recv()
    reduced = reduced_ref[...] + back_a[...].astype(F32)
    lows = []
    for h, cols, vcols in heads:
        lows.append(norm_back(key_raw_ref[:, cols], reduced[:, cols]).astype(BF16))
    key_low = jnp.concatenate(lows, axis=1)
    value_low = reduced[:, width:].astype(BF16)

    for j in range(blocks):
        rows_j = slice(j * HD, (j + 1) * HD)
        part = mm(key_low, kw_ref[rows_j, :], NT) + mm(value_low, vw_ref[rows_j, :], NT)
        parts[j] = part[:half].astype(BF16)
        parts[blocks + j] = part[half:].astype(BF16)

    def red_copy(i):
        to = lax.rem(t + i, n_tp)
        return to, pltpu.make_async_remote_copy(
            src_ref=parts.at[lax.min(to, n_red - 1)],
            dst_ref=parts_in.at[i - 1],
            send_sem=red_send.at[i - 1],
            recv_sem=red_recv.at[i - 1],
            device_id={"tp": to},
            device_id_type=MESH,
        )

    for i in range(1, n_tp):
        to, copy = red_copy(i)

        @pl.when(to < n_red)
        def _():
            copy.start()

    low = jnp.concatenate([key_low, value_low], axis=1)
    n_out = n_col // n_seq
    chips_per = n_seq // 4
    piece = chips_per * CS * n_out
    for j in range(n_col // piece):
        full = mm(lat_ref[:, j * piece : (j + 1) * piece], low, TN)
        for p in range(chips_per):
            for c in range(CS):
                start = (p * CS + c) * n_out
                prod[c, j * chips_per + p] = full[start : start + n_out].astype(BF16)

    waits = []

    def send(src, dst, index, to):
        copy = remote(src, dst, sems.at[index], recvs.at[index], to)
        copy.start()
        waits.append(copy)
        return copy

    send(prod.at[1 - core], r1, 0, partner).wait_recv()
    for xx in range(XS):
        rows_x = slice(xx * YS, (xx + 1) * YS)
        a1[xx] = (prod[core, rows_x].astype(F32) + r1[rows_x].astype(F32)).astype(BF16)
    hy = YS // 2
    c1 = send(a1.at[x_far, :hy], r2.at[0], 1, to_xu)
    c2 = send(a1.at[x_far, hy:], r2.at[1], 2, to_xd)
    c3 = send(a1.at[x_up, hy:], r3.at[hy:], 3, to_xu)
    c4 = send(a1.at[x_dn, :hy], r4.at[:hy], 4, to_xd)

    span = (REACH + 1) * n_lat
    for h, cols, vcols in heads:
        key_w = window[:, :, cols].reshape(span, HD)
        value_w = window[:, :, vcols].reshape(span, HD)
        context = mm(probs[h], value_w, TN)
        att_ref[:, cols] = (gates[:, h : h + 1] * context).astype(BF16)
        grad_hat = mm(gscores[h], key_w, TN) / scale
        gq_ref[:, cols] = norm_back(q_ref[:, cols].astype(F32), grad_hat).astype(BF16)

    c1.wait_recv()
    a1[x_up, :hy] = (a1[x_up, :hy].astype(F32) + r2[0].astype(F32)).astype(BF16)
    c5 = send(a1.at[x_up, :hy], r3.at[:hy], 5, to_xu)
    c2.wait_recv()
    a1[x_dn, hy:] = (a1[x_dn, hy:].astype(F32) + r2[1].astype(F32)).astype(BF16)
    c6 = send(a1.at[x_dn, hy:], r4.at[hy:], 6, to_xd)

    def all_copy(i):
        to = lax.rem(t + i, n_tp)
        slot = lax.min(t, n_red - 1)
        return pltpu.make_async_remote_copy(
            src_ref=result,
            dst_ref=gathered.at[slot],
            send_sem=all_send.at[i - 1],
            recv_sem=all_recv.at[slot],
            device_id={"tp": to},
            device_id_type=MESH,
        )

    def from_copy(r):
        return pltpu.make_async_remote_copy(
            src_ref=result,
            dst_ref=gathered.at[r],
            send_sem=all_send.at[0],
            recv_sem=all_recv.at[r],
            device_id={"tp": lax.rem(t + 1, n_tp)},
            device_id_type=MESH,
        )

    @pl.when(t < n_red)
    def _():
        for i in range(1, n_tp):
            red_copy(i)[1].wait_recv()
        total = parts[lax.min(t, n_red - 1)].astype(F32)
        for i in range(n_tp - 1):
            total = total + parts_in[i].astype(F32)
        result[...] = total.astype(BF16)
        for i in range(1, n_tp):
            all_copy(i).start()

    c3.wait_recv()
    c4.wait_recv()
    c5.wait_recv()
    c6.wait_recv()
    for yy in range(YS):
        value = a1[x, yy].astype(F32) + r3[yy].astype(F32) + r4[yy].astype(F32)
        a2[yy, 0] = value[:, :width].astype(BF16)
        a2[yy, 1] = value[:, width:].astype(BF16)
    d1 = send(a2.at[y_far, 0], u2.at[0], 7, to_yu)
    d2 = send(a2.at[y_far, 1], u2.at[1], 8, to_yd)
    d3 = send(a2.at[y_up, 1], u3.at[1], 9, to_yu)
    d4 = send(a2.at[y_dn, 0], u4.at[0], 10, to_yd)
    d1.wait_recv()
    a2[y_up, 0] = (a2[y_up, 0].astype(F32) + u2[0].astype(F32)).astype(BF16)
    d5 = send(a2.at[y_up, 0], u3.at[0], 11, to_yu)
    d2.wait_recv()
    a2[y_dn, 1] = (a2[y_dn, 1].astype(F32) + u2[1].astype(F32)).astype(BF16)
    d6 = send(a2.at[y_dn, 1], u4.at[1], 12, to_yd)
    for copy in (d3, d4, d5, d6):
        copy.wait_recv()
    for i in range(2):
        wsum_ref[i] = a2[y, i].astype(F32) + u3[i].astype(F32) + u4[i].astype(F32)

    for r in range(n_red):

        @pl.when(t != r)
        def _():
            from_copy(r).wait_recv()

    for copy in waits:
        copy.wait_send()
    pass_a.wait_send()
    pass_c.wait_send()
    pass_d0.wait_send()
    give_c.wait_send()
    give_d.wait_send()
    give_a.wait_send()

    @pl.when(core == 0)
    def _():
        pass_b.wait_send()
        give_e.wait_send()

    @pl.when(core == 1)
    def _():
        pass_e.wait_send()
        give_b.wait_send()

    for i in range(1, n_tp):
        to, copy = red_copy(i)

        @pl.when(to < n_red)
        def _():
            copy.wait_send()

    @pl.when(t < n_red)
    def _():
        for i in range(1, n_tp):
            all_copy(i).wait_send()
        gathered[lax.min(t, n_red - 1)] = result[...]


def finish_kernel(
    att_in, gq_in, resampled_ref, gathered, wsum_ref, att_ref, gq_ref, glat_ref, gk_ref, gv_ref
):
    att_ref[...] = att_in[...]
    gq_ref[...] = gq_in[...]
    gk_ref[...] = wsum_ref[0]
    gv_ref[...] = wsum_ref[1]
    half = gathered.shape[1]
    blocks = gathered.shape[0] // 2
    for k in range(2):
        rows = slice(k * half, (k + 1) * half)
        grad = jnp.concatenate(
            [gathered[k * blocks + j].astype(F32) for j in range(blocks)], axis=1
        )
        glat_ref[rows, :] = norm_back(resampled_ref[rows, :], grad)


def on_device(
    queries,
    cotangent,
    gate,
    token_image,
    patches,
    patch_count,
    latents,
    latent_queries,
    rs_key,
    rs_value,
    rs_out,
    key_weight,
    value_weight,
):
    n_seq = lax.axis_size("seq")
    n_tp = lax.axis_size("tp")
    width = key_weight.shape[1]
    tokens = queries.shape[0]
    n_lat, n_col = latents.shape
    n_patch = patches.shape[1]
    inner = latent_queries.shape[1]
    rows = n_patch + n_lat
    heads = width // HD
    span = (REACH + 1) * n_lat
    n_red = 2 * (n_col // HD)
    n_out = n_col // n_seq
    half = n_lat // 2
    vmem = pl.BlockSpec(memory_space=pltpu.VMEM)
    smem = pl.BlockSpec(memory_space=pltpu.SMEM)
    anywhere = pl.BlockSpec(memory_space=pl.ANY)
    dma = pltpu.SemaphoreType.DMA
    slot = (n_lat, 2 * width)
    bulk = (
        patches[0],
        rs_key,
        rs_value,
        rs_out,
        key_weight,
        value_weight,
        queries,
        cotangent,
    )
    middle = pl.pallas_call(
        functools.partial(whole_kernel, n_seq, n_tp, n_red),
        name="whole",
        out_shape=(
            jax.ShapeDtypeStruct((tokens, width), BF16),
            jax.ShapeDtypeStruct((tokens, width), BF16),
            jax.ShapeDtypeStruct((n_lat, n_col), F32),
            jax.ShapeDtypeStruct((n_red, half, HD), BF16),
            jax.ShapeDtypeStruct((2, n_out, width), F32),
        ),
        in_specs=[smem] + [vmem] * 4 + [anywhere] * 8,
        out_specs=(vmem,) * 5,
        scratch_shapes=[pltpu.VMEM(a.shape, a.dtype) for a in bulk]
        + [
            pltpu.VMEM((rows, n_col), BF16),
            pltpu.VMEM((rows, inner), F32),
            pltpu.VMEM((rows, inner), F32),
            pltpu.VMEM((n_lat, n_col), BF16),
            pltpu.VMEM((n_lat, width), F32),
            pltpu.VMEM((REACH + 1,) + slot, BF16),
            pltpu.VMEM((tokens, width), BF16),
            pltpu.VMEM((tokens, width), BF16),
            pltpu.VMEM((heads, span, tokens), BF16),
            pltpu.VMEM((heads, span, tokens), BF16),
            pltpu.VMEM((REACH + 1,) + slot, F32),
            pltpu.VMEM((REACH,) + slot, BF16),
            pltpu.VMEM(slot, BF16),
            pltpu.VMEM(slot, BF16),
            pltpu.VMEM(slot, BF16),
            pltpu.VMEM(slot, BF16),
            pltpu.VMEM(slot, BF16),
            pltpu.VMEM(slot, F32),
            pltpu.VMEM((n_red, half, HD), BF16),
            pltpu.VMEM((n_tp - 1, half, HD), BF16),
            pltpu.VMEM((half, HD), BF16),
            pltpu.VMEM((CS, XS * YS, n_out, 2 * width), BF16),
            pltpu.VMEM((XS * YS, n_out, 2 * width), BF16),
            pltpu.VMEM((XS, YS, n_out, 2 * width), BF16),
            pltpu.VMEM((2, YS // 2, n_out, 2 * width), BF16),
            pltpu.VMEM((YS, n_out, 2 * width), BF16),
            pltpu.VMEM((YS, n_out, 2 * width), BF16),
            pltpu.VMEM((YS, 2, n_out, width), BF16),
            pltpu.VMEM((2, n_out, width), BF16),
            pltpu.VMEM((2, n_out, width), BF16),
            pltpu.VMEM((2, n_out, width), BF16),
            dma((8,)),
            dma((5,)),
            dma((4,)),
            dma((5,)),
            dma((5,)),
            dma((n_tp - 1,)),
            dma((n_tp - 1,)),
            dma((n_tp - 1,)),
            dma((n_red,)),
            dma((13,)),
            dma((13,)),
        ],
        compiler_params=pltpu.CompilerParams(collective_id=0, has_side_effects=True),
    )(
        patch_count,
        latents,
        latent_queries,
        gate.reshape(1, heads),
        token_image.reshape(1, tokens),
        *bulk,
    )
    attended, grad_query, grad_latents, grad_key_weight, grad_value_weight = pl.pallas_call(
        finish_kernel,
        name="finish",
        out_shape=(
            jax.ShapeDtypeStruct((tokens, width), BF16),
            jax.ShapeDtypeStruct((tokens, width), BF16),
            jax.ShapeDtypeStruct((n_lat, n_col), F32),
            jax.ShapeDtypeStruct((n_out, width), F32),
            jax.ShapeDtypeStruct((n_out, width), F32),
        ),
        in_specs=[vmem] * 5,
        out_specs=(vmem,) * 5,
    )(*middle)
    return (attended, grad_query, grad_latents[None], grad_key_weight, grad_value_weight)


def solution(mesh):
    placed = (
        P("seq", "tp"),
        P("seq", "tp"),
        P("tp"),
        P("seq"),
        P("seq", None, None),
        P("seq"),
        P(),
        P(),
        P(),
        P(),
        P(),
        P(None, "tp"),
        P(None, "tp"),
    )
    return jax.shard_map(
        on_device,
        mesh=mesh,
        in_specs=placed,
        out_specs=(
            P("seq", "tp"),
            P("seq", "tp"),
            P("seq", None, None),
            P("seq", "tp"),
            P("seq", "tp"),
        ),
        check_vma=False,
    )
```

```python
import functools

import jax
import jax.numpy as jnp
from jax import lax
from jax.experimental import pallas as pl
from jax.experimental.pallas import tpu as pltpu
from jax.sharding import PartitionSpec as P

HD = 128
RHD = 96
REACH = 4
EPS = 1e-05
XS, YS, CS = 4, 4, 2
MESH = pl.DeviceIdType.MESH
F32 = jnp.float32
BF16 = jnp.bfloat16
NT = (((1,), (1,)), ((), ()))
TN = (((0,), (0,)), ((), ()))


def mm(a, b, dims=(((1,), (0,)), ((), ()))):
    return lax.dot_general(a, b, dims, preferred_element_type=F32)


def norm_stats(matrix):
    average = jnp.mean(matrix, axis=-1, keepdims=True)
    centered = matrix - average
    variance = jnp.mean(centered * centered, axis=-1, keepdims=True)
    inverse = lax.rsqrt(variance + EPS)
    return centered * inverse, inverse


def norm_rows(matrix):
    return norm_stats(matrix.astype(F32))[0]


def norm_back(matrix, incoming):
    normed, inverse = norm_stats(matrix)
    first_mean = jnp.mean(incoming, axis=-1, keepdims=True)
    second_mean = jnp.mean(incoming * normed, axis=-1, keepdims=True)
    return inverse * (incoming - first_mean - normed * second_mean)


def whole_kernel(
    n_seq,
    n_tp,
    n_red,
    count_ref,
    latents_ref,
    lq_ref,
    gate_ref,
    image_ref,
    patches_hbm,
    rs_key_hbm,
    rs_value_hbm,
    rs_out_hbm,
    kw_hbm,
    vw_hbm,
    q_hbm,
    cot_hbm,
    att_ref,
    gq_ref,
    resampled_ref,
    gathered,
    wsum_ref,
    patches_ref,
    rs_key_ref,
    rs_value_ref,
    rs_out_ref,
    kw_ref,
    vw_ref,
    q_ref,
    cot_ref,
    inputs,
    keys,
    values,
    lat_ref,
    lat_t,
    key_raw_ref,
    window,
    text,
    grad_ctx,
    probs,
    gscores,
    terms,
    terms_low,
    back_e,
    back_c,
    back_d,
    back_b,
    back_a,
    reduced_ref,
    parts,
    parts_in,
    result,
    prod,
    r1,
    a1,
    r2,
    r3,
    r4,
    a2,
    u2,
    u3,
    u4,
    load_sem,
    win_send,
    win_recv,
    back_send,
    back_recv,
    red_send,
    red_recv,
    all_send,
    all_recv,
    sems,
    recvs,
):
    s = lax.axis_index("seq")
    t = lax.axis_index("tp")
    width = kw_ref.shape[1]
    n_lat, n_col = lat_ref.shape
    half = n_lat // 2
    blocks = n_col // HD
    tokens = q_ref.shape[0]
    core = lax.rem(s, CS)
    chip = lax.div(s, CS)
    y = lax.rem(chip, YS)
    x = lax.div(chip, YS)

    def seq_of(xx, yy, cc):
        return (xx * YS + yy) * CS + cc

    partner = seq_of(x, y, 1 - core)
    ahead, behind = lax.rem(s + CS, n_seq), lax.rem(s + n_seq - CS, n_seq)
    x_up, x_dn, x_far = lax.rem(x + 1, XS), lax.rem(x + XS - 1, XS), lax.rem(x + 2, XS)
    y_up, y_dn, y_far = lax.rem(y + 1, YS), lax.rem(y + YS - 1, YS), lax.rem(y + 2, YS)
    to_xu, to_xd = seq_of(x_up, y, core), seq_of(x_dn, y, core)
    to_yu, to_yd = seq_of(x, y_up, core), seq_of(x, y_dn, core)

    loads = []
    for i, (src, dst) in enumerate(
        (
            (patches_hbm, patches_ref),
            (rs_key_hbm, rs_key_ref),
            (rs_value_hbm, rs_value_ref),
            (rs_out_hbm, rs_out_ref),
            (kw_hbm, kw_ref),
            (vw_hbm, vw_ref),
            (q_hbm, q_ref),
            (cot_hbm, cot_ref),
        )
    ):
        load = pltpu.make_async_copy(src, dst, load_sem.at[i])
        load.start()
        loads.append(load)

    barrier = pltpu.get_barrier_semaphore()
    friends = [partner, ahead, behind, to_xu, to_xd, to_yu, to_yd]
    for other in friends:
        pl.semaphore_signal(barrier, inc=1, device_id={"seq": other}, device_id_type=MESH)
    for i in range(1, n_tp):
        pl.semaphore_signal(
            barrier, inc=1, device_id={"tp": lax.rem(t + i, n_tp)}, device_id_type=MESH
        )

    n_patch = patches_ref.shape[0]
    rows = n_patch + n_lat
    inputs[n_patch:, :] = norm_rows(latents_ref[...]).astype(BF16)
    loads[0].wait()
    for r in range(0, n_patch, 64):
        inputs[r : r + 64, :] = norm_rows(patches_ref[r : r + 64, :]).astype(BF16)
    loads[1].wait()
    keys[...] = mm(inputs[...], rs_key_ref[...])
    loads[2].wait()
    values[...] = mm(inputs[...], rs_value_ref[...])
    loads[3].wait()
    position = lax.broadcasted_iota(jnp.int32, (n_lat, rows), 1)
    kept = jnp.logical_or(position < count_ref[0], position >= n_patch)
    total = latents_ref[...].astype(F32)
    queries = lq_ref[...].astype(F32)
    for h in range(lq_ref.shape[1] // RHD):
        cols = slice(h * RHD, (h + 1) * RHD)
        key_h = norm_rows(keys[:, cols]).astype(BF16)
        query_h = norm_rows(queries[:, cols]).astype(BF16)
        scores = mm(query_h, key_h, NT) / RHD**0.5
        weights = jnp.where(kept, jnp.exp(scores), 0.0)
        prob = (weights / jnp.sum(weights, axis=-1, keepdims=True)).astype(BF16)
        context = mm(prob, values[:, cols].astype(BF16)).astype(BF16)
        total = total + mm(context, rs_out_ref[cols, :])
    resampled_ref[...] = total
    lat = norm_rows(total).astype(BF16)
    lat_ref[...] = lat
    loads[4].wait()
    key_raw = mm(lat, kw_ref[...])
    key_raw_ref[...] = key_raw
    for h in range(width // HD):
        cols = slice(h * HD, (h + 1) * HD)
        window[REACH, 0, :, cols] = norm_rows(key_raw[:, cols]).astype(BF16)

    pl.semaphore_wait(barrier, len(friends) + n_tp - 1)

    def remote(src, dst, send_sem, recv_sem, to):
        return pltpu.make_async_remote_copy(
            src_ref=src,
            dst_ref=dst,
            send_sem=send_sem,
            recv_sem=recv_sem,
            device_id={"seq": to},
            device_id_type=MESH,
        )

    def pass_on(k_from, k_to, index, to):
        return [
            remote(
                window.at[k_from, g],
                window.at[k_to, g],
                win_send.at[2 * index + g],
                win_recv.at[2 * k_to + g],
                to,
            )
            for g in range(2)
        ]

    pass_a = pass_on(4, 2, 0, ahead)
    pass_b = pass_on(4, 3, 1, partner)
    pass_c = pass_on(2, 0, 2, ahead)
    pass_d0 = pass_on(2, 1, 3, partner)
    pass_d1 = pass_on(2, 3, 3, partner)
    pass_e = pass_on(0, 1, 4, partner)

    def send_own(g):
        pass_a[g].start()

        @pl.when(core == 0)
        def _():
            pass_b[g].start()

    def relay_first(g):
        pass_a[g].wait_recv()
        pass_c[g].start()

        @pl.when(core == 0)
        def _():
            pass_d0[g].start()

        @pl.when(core == 1)
        def _():
            pass_d1[g].start()

    def relay_second(g):
        pass_c[g].wait_recv()

        @pl.when(core == 1)
        def _():
            pass_e[g].start()

    send_own(0)
    loads[5].wait()
    window[REACH, 1] = mm(lat, vw_ref[...]).astype(BF16)
    send_own(1)

    gates = jnp.tanh(gate_ref[...])
    scale = HD**0.5
    loads[6].wait()
    loads[7].wait()
    heads = []
    for h in range(width // HD):
        cols = slice(h * HD, (h + 1) * HD)
        heads.append((h, cols))
        text[:, cols] = norm_rows(q_ref[:, cols]).astype(BF16)
        grad_ctx[:, cols] = (gates[:, h : h + 1] * cot_ref[:, cols].astype(F32)).astype(BF16)
    image = image_ref[...]

    def attend(k):
        match = image == s - REACH + k
        other = jnp.where(match, 0.0, 1.0)
        lat_rows = slice(k * n_lat, (k + 1) * n_lat)
        for h, cols in heads:
            scores = mm(window[k, 0, :, cols], text[:, cols], NT) / scale
            weights = jnp.where(match, jnp.exp(scores), 0.0)
            prob = weights / (jnp.sum(weights, axis=0, keepdims=True) + other)
            low = prob.astype(BF16)
            grad_prob = mm(window[k, 1, :, cols], grad_ctx[:, cols], NT)
            inner = jnp.sum(prob * grad_prob, axis=0, keepdims=True)
            grad_score = (prob * (grad_prob - inner)).astype(BF16)
            probs[h, lat_rows, :] = low
            gscores[h, lat_rows, :] = grad_score
            terms[k, 0, :, cols] = mm(grad_score, text[:, cols]) / scale
            terms[k, 1, :, cols] = mm(low, grad_ctx[:, cols])

    attend(4)
    relay_first(0)
    relay_first(1)
    lat_columns = jnp.transpose(lat_ref[...].astype(F32))
    n_out = n_col // n_seq
    for p in range(XS * YS):
        for c in range(CS):
            start = (p * CS + c) * n_out
            slot_rows = slice(p % YS * n_out, (p % YS + 1) * n_out)
            lat_t[c, p // YS, slot_rows, :] = lat_columns[start : start + n_out]
    attend(2)
    for g in range(2):
        pass_b[g].wait_recv()
    attend(3)
    terms_low[3] = terms[3].astype(BF16)
    relay_second(0)
    relay_second(1)
    attend(0)
    for g in range(2):
        pass_e[g].wait_recv()
    attend(1)
    terms_low[1] = terms[1].astype(BF16)

    def give(k, dst, index, to):
        return [
            remote(
                terms_low.at[k, g],
                dst.at[g],
                back_send.at[2 * index + g],
                back_recv.at[2 * index + g],
                to,
            )
            for g in range(2)
        ]

    give_e = give(1, back_e, 0, partner)
    give_c = give(0, back_c, 1, behind)
    give_d = give(3 - 2 * core, back_d, 2, partner)
    give_b = give(3, back_b, 3, partner)
    give_a = give(2, back_a, 4, behind)

    @pl.when(core == 0)
    def _():
        give_e[0].start()
        give_e[1].start()
        terms_low[0] = terms[0].astype(BF16)

    for g in range(2):

        @pl.when(core == 1)
        def _():
            give_e[g].wait_recv()
            terms_low[0, g] = (terms[0, g] + back_e[g].astype(F32)).astype(BF16)

        give_c[g].start()
        give_d[g].start()

    @pl.when(core == 1)
    def _():
        give_b[0].start()
        give_b[1].start()

    for g in range(2):
        give_d[g].wait_recv()
        near = terms[2, g] + back_d[g].astype(F32)
        give_c[g].wait_recv()
        terms_low[2, g] = (near + back_c[g].astype(F32)).astype(BF16)
        give_a[g].start()

    reduced_ref[...] = terms[REACH]

    @pl.when(core == 0)
    def _():
        for g in range(2):
            give_b[g].wait_recv()
            reduced_ref[g] += back_b[g].astype(F32)

    give_a[0].wait_recv()
    reduced = reduced_ref[0] + back_a[0].astype(F32)
    lows = []
    for h, cols in heads:
        lows.append(norm_back(key_raw_ref[:, cols], reduced[:, cols]).astype(BF16))
    key_low = jnp.concatenate(lows, axis=1)
    give_a[1].wait_recv()
    value_low = (reduced_ref[1] + back_a[1].astype(F32)).astype(BF16)

    for j in range(blocks):
        rows_j = slice(j * HD, (j + 1) * HD)
        part = mm(key_low, kw_ref[rows_j, :], NT) + mm(value_low, vw_ref[rows_j, :], NT)
        parts[j] = part[:half].astype(BF16)
        parts[blocks + j] = part[half:].astype(BF16)

    def red_copy(i):
        to = lax.rem(t + i, n_tp)
        return to, pltpu.make_async_remote_copy(
            src_ref=parts.at[lax.min(to, n_red - 1)],
            dst_ref=parts_in.at[i - 1],
            send_sem=red_send.at[i - 1],
            recv_sem=red_recv.at[i - 1],
            device_id={"tp": to},
            device_id_type=MESH,
        )

    far_first = sorted(range(1, n_tp), key=lambda i: -min(i, n_tp - i))
    for i in far_first:
        to, copy = red_copy(i)

        @pl.when(to < n_red)
        def _():
            copy.start()

    low = jnp.concatenate([key_low, value_low], axis=1)
    waits = []

    def send(src, dst, index, to):
        copy = remote(src, dst, sems.at[index], recvs.at[index], to)
        copy.start()
        waits.append(copy)
        return copy

    def product(c, xx):
        full = mm(lat_t[c, xx].astype(BF16), low)
        return full.reshape(YS, n_out, 2 * width)

    order = (x_far, x_up, x_dn, x)
    swaps = []
    for i, xx in enumerate(order):
        prod[xx] = product(1 - core, xx).astype(BF16)
        swaps.append(send(prod.at[xx], r1.at[xx], 13 + i, partner))
    hy = YS // 2
    for i, xx in enumerate(order):
        mine = product(core, xx)
        swaps[i].wait_recv()
        a1[xx] = (mine + r1[xx].astype(F32)).astype(BF16)
        if i == 0:
            c1 = send(a1.at[x_far, :hy], r2.at[0], 1, to_xu)
            c2 = send(a1.at[x_far, hy:], r2.at[1], 2, to_xd)
        if i == 1:
            c3 = send(a1.at[x_up, hy:], r3.at[hy:], 3, to_xu)
        if i == 2:
            c4 = send(a1.at[x_dn, :hy], r4.at[:hy], 4, to_xd)

    span = (REACH + 1) * n_lat
    for h, cols in heads:
        key_w = window[:, 0, :, cols].reshape(span, HD)
        value_w = window[:, 1, :, cols].reshape(span, HD)
        context = mm(probs[h], value_w, TN)
        att_ref[:, cols] = (gates[:, h : h + 1] * context).astype(BF16)
        grad_hat = mm(gscores[h], key_w, TN) / scale
        gq_ref[:, cols] = norm_back(q_ref[:, cols].astype(F32), grad_hat).astype(BF16)

    c1.wait_recv()
    a1[x_up, :hy] = (a1[x_up, :hy].astype(F32) + r2[0].astype(F32)).astype(BF16)
    c5 = send(a1.at[x_up, :hy], r3.at[:hy], 5, to_xu)
    c2.wait_recv()
    a1[x_dn, hy:] = (a1[x_dn, hy:].astype(F32) + r2[1].astype(F32)).astype(BF16)
    c6 = send(a1.at[x_dn, hy:], r4.at[hy:], 6, to_xd)

    def all_copy(i):
        to = lax.rem(t + i, n_tp)
        slot = lax.min(t, n_red - 1)
        return pltpu.make_async_remote_copy(
            src_ref=result,
            dst_ref=gathered.at[slot],
            send_sem=all_send.at[i - 1],
            recv_sem=all_recv.at[slot],
            device_id={"tp": to},
            device_id_type=MESH,
        )

    def from_copy(r):
        return pltpu.make_async_remote_copy(
            src_ref=result,
            dst_ref=gathered.at[r],
            send_sem=all_send.at[0],
            recv_sem=all_recv.at[r],
            device_id={"tp": lax.rem(t + 1, n_tp)},
            device_id_type=MESH,
        )

    @pl.when(t < n_red)
    def _():
        for i in range(1, n_tp):
            red_copy(i)[1].wait_recv()
        total = parts[lax.min(t, n_red - 1)].astype(F32)
        for i in range(n_tp - 1):
            total = total + parts_in[i].astype(F32)
        result[...] = total.astype(BF16)
        for i in far_first:
            all_copy(i).start()

    c3.wait_recv()
    c4.wait_recv()
    c5.wait_recv()
    c6.wait_recv()
    for yy in range(YS):
        value = a1[x, yy].astype(F32) + r3[yy].astype(F32) + r4[yy].astype(F32)
        a2[yy, 0] = value[:, :width].astype(BF16)
        a2[yy, 1] = value[:, width:].astype(BF16)
    d1 = send(a2.at[y_far, 0], u2.at[0], 7, to_yu)
    d2 = send(a2.at[y_far, 1], u2.at[1], 8, to_yd)
    d3 = send(a2.at[y_up, 1], u3.at[1], 9, to_yu)
    d4 = send(a2.at[y_dn, 0], u4.at[0], 10, to_yd)
    d1.wait_recv()
    a2[y_up, 0] = (a2[y_up, 0].astype(F32) + u2[0].astype(F32)).astype(BF16)
    d5 = send(a2.at[y_up, 0], u3.at[0], 11, to_yu)
    d2.wait_recv()
    a2[y_dn, 1] = (a2[y_dn, 1].astype(F32) + u2[1].astype(F32)).astype(BF16)
    d6 = send(a2.at[y_dn, 1], u4.at[1], 12, to_yd)
    for copy in (d3, d4, d5, d6):
        copy.wait_recv()
    for i in range(2):
        wsum_ref[i] = a2[y, i].astype(F32) + u3[i].astype(F32) + u4[i].astype(F32)

    for r in range(n_red):

        @pl.when(t != r)
        def _():
            from_copy(r).wait_recv()

    for copy in waits:
        copy.wait_send()
    for g in range(2):
        for copies in (pass_a, pass_c, pass_d0, give_c, give_d, give_a):
            copies[g].wait_send()

    @pl.when(core == 0)
    def _():
        for g in range(2):
            pass_b[g].wait_send()
            give_e[g].wait_send()

    @pl.when(core == 1)
    def _():
        for g in range(2):
            pass_e[g].wait_send()
            give_b[g].wait_send()

    for i in range(1, n_tp):
        to, copy = red_copy(i)

        @pl.when(to < n_red)
        def _():
            copy.wait_send()

    @pl.when(t < n_red)
    def _():
        for i in range(1, n_tp):
            all_copy(i).wait_send()
        gathered[lax.min(t, n_red - 1)] = result[...]


def finish_kernel(
    att_in, gq_in, resampled_ref, gathered, wsum_ref, att_ref, gq_ref, glat_ref, gk_ref, gv_ref
):
    att_ref[...] = att_in[...]
    gq_ref[...] = gq_in[...]
    gk_ref[...] = wsum_ref[0]
    gv_ref[...] = wsum_ref[1]
    half = gathered.shape[1]
    blocks = gathered.shape[0] // 2
    for k in range(2):
        rows = slice(k * half, (k + 1) * half)
        grad = jnp.concatenate(
            [gathered[k * blocks + j].astype(F32) for j in range(blocks)], axis=1
        )
        glat_ref[rows, :] = norm_back(resampled_ref[rows, :], grad)


def on_device(
    queries,
    cotangent,
    gate,
    token_image,
    patches,
    patch_count,
    latents,
    latent_queries,
    rs_key,
    rs_value,
    rs_out,
    key_weight,
    value_weight,
):
    n_seq = lax.axis_size("seq")
    n_tp = lax.axis_size("tp")
    width = key_weight.shape[1]
    tokens = queries.shape[0]
    n_lat, n_col = latents.shape
    n_patch = patches.shape[1]
    inner = latent_queries.shape[1]
    rows = n_patch + n_lat
    heads = width // HD
    span = (REACH + 1) * n_lat
    n_red = 2 * (n_col // HD)
    n_out = n_col // n_seq
    half = n_lat // 2
    vmem = pl.BlockSpec(memory_space=pltpu.VMEM)
    smem = pl.BlockSpec(memory_space=pltpu.SMEM)
    anywhere = pl.BlockSpec(memory_space=pl.ANY)
    dma = pltpu.SemaphoreType.DMA
    slot = (2, n_lat, width)
    bulk = (
        patches[0],
        rs_key,
        rs_value,
        rs_out,
        key_weight,
        value_weight,
        queries,
        cotangent,
    )
    middle = pl.pallas_call(
        functools.partial(whole_kernel, n_seq, n_tp, n_red),
        name="whole",
        out_shape=(
            jax.ShapeDtypeStruct((tokens, width), BF16),
            jax.ShapeDtypeStruct((tokens, width), BF16),
            jax.ShapeDtypeStruct((n_lat, n_col), F32),
            jax.ShapeDtypeStruct((n_red, half, HD), BF16),
            jax.ShapeDtypeStruct((2, n_out, width), F32),
        ),
        in_specs=[smem] + [vmem] * 4 + [anywhere] * 8,
        out_specs=(vmem,) * 5,
        scratch_shapes=[pltpu.VMEM(a.shape, a.dtype) for a in bulk]
        + [
            pltpu.VMEM((rows, n_col), BF16),
            pltpu.VMEM((rows, inner), F32),
            pltpu.VMEM((rows, inner), F32),
            pltpu.VMEM((n_lat, n_col), BF16),
            pltpu.VMEM((CS, XS, YS * n_out, n_lat), F32),
            pltpu.VMEM((n_lat, width), F32),
            pltpu.VMEM((REACH + 1,) + slot, BF16),
            pltpu.VMEM((tokens, width), BF16),
            pltpu.VMEM((tokens, width), BF16),
            pltpu.VMEM((heads, span, tokens), BF16),
            pltpu.VMEM((heads, span, tokens), BF16),
            pltpu.VMEM((REACH + 1,) + slot, F32),
            pltpu.VMEM((REACH,) + slot, BF16),
            pltpu.VMEM(slot, BF16),
            pltpu.VMEM(slot, BF16),
            pltpu.VMEM(slot, BF16),
            pltpu.VMEM(slot, BF16),
            pltpu.VMEM(slot, BF16),
            pltpu.VMEM(slot, F32),
            pltpu.VMEM((n_red, half, HD), BF16),
            pltpu.VMEM((n_tp - 1, half, HD), BF16),
            pltpu.VMEM((half, HD), BF16),
            pltpu.VMEM((XS, YS, n_out, 2 * width), BF16),
            pltpu.VMEM((XS, YS, n_out, 2 * width), BF16),
            pltpu.VMEM((XS, YS, n_out, 2 * width), BF16),
            pltpu.VMEM((2, YS // 2, n_out, 2 * width), BF16),
            pltpu.VMEM((YS, n_out, 2 * width), BF16),
            pltpu.VMEM((YS, n_out, 2 * width), BF16),
            pltpu.VMEM((YS, 2, n_out, width), BF16),
            pltpu.VMEM((2, n_out, width), BF16),
            pltpu.VMEM((2, n_out, width), BF16),
            pltpu.VMEM((2, n_out, width), BF16),
            dma((8,)),
            dma((10,)),
            dma((8,)),
            dma((10,)),
            dma((10,)),
            dma((n_tp - 1,)),
            dma((n_tp - 1,)),
            dma((n_tp - 1,)),
            dma((n_red,)),
            dma((17,)),
            dma((17,)),
        ],
        compiler_params=pltpu.CompilerParams(collective_id=0, has_side_effects=True),
    )(
        patch_count,
        latents,
        latent_queries,
        gate.reshape(1, heads),
        token_image.reshape(1, tokens),
        *bulk,
    )
    attended, grad_query, grad_latents, grad_key_weight, grad_value_weight = pl.pallas_call(
        finish_kernel,
        name="finish",
        out_shape=(
            jax.ShapeDtypeStruct((tokens, width), BF16),
            jax.ShapeDtypeStruct((tokens, width), BF16),
            jax.ShapeDtypeStruct((n_lat, n_col), F32),
            jax.ShapeDtypeStruct((n_out, width), F32),
            jax.ShapeDtypeStruct((n_out, width), F32),
        ),
        in_specs=[vmem] * 5,
        out_specs=(vmem,) * 5,
    )(*middle)
    return (attended, grad_query, grad_latents[None], grad_key_weight, grad_value_weight)


def solution(mesh):
    placed = (
        P("seq", "tp"),
        P("seq", "tp"),
        P("tp"),
        P("seq"),
        P("seq", None, None),
        P("seq"),
        P(),
        P(),
        P(),
        P(),
        P(),
        P(None, "tp"),
        P(None, "tp"),
    )
    return jax.shard_map(
        on_device,
        mesh=mesh,
        in_specs=placed,
        out_specs=(
            P("seq", "tp"),
            P("seq", "tp"),
            P("seq", None, None),
            P("seq", "tp"),
            P("seq", "tp"),
        ),
        check_vma=False,
    )
```

```python
import functools

import jax
import jax.numpy as jnp
from jax import lax
from jax.experimental import pallas as pl
from jax.experimental.pallas import tpu as pltpu
from jax.sharding import PartitionSpec as P

HD = 128
RHD = 96
REACH = 4
EPS = 1e-05
XS, YS, CS = 4, 4, 2
MESH = pl.DeviceIdType.MESH
F32 = jnp.float32
BF16 = jnp.bfloat16
NT = (((1,), (1,)), ((), ()))
TN = (((0,), (0,)), ((), ()))


def mm(a, b, dims=(((1,), (0,)), ((), ()))):
    return lax.dot_general(a, b, dims, preferred_element_type=F32)


def norm_stats(matrix):
    average = jnp.mean(matrix, axis=-1, keepdims=True)
    centered = matrix - average
    variance = jnp.mean(centered * centered, axis=-1, keepdims=True)
    inverse = lax.rsqrt(variance + EPS)
    return centered * inverse, inverse


def norm_rows(matrix):
    return norm_stats(matrix.astype(F32))[0]


def norm_back(matrix, incoming):
    normed, inverse = norm_stats(matrix)
    first_mean = jnp.mean(incoming, axis=-1, keepdims=True)
    second_mean = jnp.mean(incoming * normed, axis=-1, keepdims=True)
    return inverse * (incoming - first_mean - normed * second_mean)


def whole_kernel(
    n_seq,
    n_tp,
    n_red,
    count_ref,
    latents_ref,
    lq_ref,
    gate_ref,
    image_ref,
    patches_hbm,
    rs_key_hbm,
    rs_value_hbm,
    rs_out_hbm,
    kw_hbm,
    vw_hbm,
    q_hbm,
    cot_hbm,
    att_hbm,
    gq_hbm,
    resampled_hbm,
    gathered,
    wsum_ref,
    att_ref,
    gq_ref,
    resampled_ref,
    patches_ref,
    rs_key_ref,
    rs_value_ref,
    rs_out_ref,
    kw_ref,
    vw_ref,
    q_ref,
    cot_ref,
    inputs,
    query_hat,
    keys_t,
    values_t,
    context_t,
    lat_ref,
    lat_t,
    key_raw_ref,
    window,
    text,
    grad_ctx,
    probs,
    gscores,
    terms,
    terms_low,
    back_e,
    back_c,
    back_d,
    back_b,
    back_a,
    reduced_ref,
    parts,
    parts_in,
    result,
    prod,
    r1,
    a1,
    r2,
    r3,
    r4,
    a2,
    u2,
    u3,
    u4,
    out_sem,
    load_sem,
    win_send,
    win_recv,
    back_send,
    back_recv,
    red_send,
    red_recv,
    all_send,
    all_recv,
    sems,
    recvs,
):
    s = lax.axis_index("seq")
    t = lax.axis_index("tp")
    width = kw_ref.shape[1]
    n_lat, n_col = lat_ref.shape
    half = n_lat // 2
    blocks = n_col // HD
    tokens = q_ref.shape[0]
    core = lax.rem(s, CS)
    chip = lax.div(s, CS)
    y = lax.rem(chip, YS)
    x = lax.div(chip, YS)

    def seq_of(xx, yy, cc):
        return (xx * YS + yy) * CS + cc

    partner = seq_of(x, y, 1 - core)
    ahead, behind = lax.rem(s + CS, n_seq), lax.rem(s + n_seq - CS, n_seq)
    x_up, x_dn, x_far = lax.rem(x + 1, XS), lax.rem(x + XS - 1, XS), lax.rem(x + 2, XS)
    y_up, y_dn, y_far = lax.rem(y + 1, YS), lax.rem(y + YS - 1, YS), lax.rem(y + 2, YS)
    to_xu, to_xd = seq_of(x_up, y, core), seq_of(x_dn, y, core)
    to_yu, to_yd = seq_of(x, y_up, core), seq_of(x, y_dn, core)

    loads = []
    for i, (src, dst) in enumerate(
        (
            (patches_hbm, patches_ref),
            (rs_key_hbm, rs_key_ref),
            (rs_value_hbm, rs_value_ref),
            (rs_out_hbm, rs_out_ref),
            (kw_hbm, kw_ref),
            (vw_hbm, vw_ref),
            (q_hbm, q_ref),
            (cot_hbm, cot_ref),
        )
    ):
        load = pltpu.make_async_copy(src, dst, load_sem.at[i])
        load.start()
        loads.append(load)

    barrier = pltpu.get_barrier_semaphore()
    friends = [partner, ahead, behind, to_xu, to_xd, to_yu, to_yd]
    for other in friends:
        pl.semaphore_signal(barrier, inc=1, device_id={"seq": other}, device_id_type=MESH)
    for i in range(1, n_tp):
        pl.semaphore_signal(
            barrier, inc=1, device_id={"tp": lax.rem(t + i, n_tp)}, device_id_type=MESH
        )

    n_patch = patches_ref.shape[0]
    rows = n_patch + n_lat
    inputs[n_patch:, :] = norm_rows(latents_ref[...]).astype(BF16)
    queries = lq_ref[...].astype(F32)
    rs_heads = range(lq_ref.shape[1] // RHD)
    for h in rs_heads:
        query_hat[h] = norm_rows(queries[:, h * RHD : (h + 1) * RHD]).astype(BF16)
    loads[0].wait()
    for r in range(0, n_patch, 64):
        inputs[r : r + 64, :] = norm_rows(patches_ref[r : r + 64, :]).astype(BF16)
    loads[1].wait()
    keys_t[...] = jnp.transpose(mm(inputs[...], rs_key_ref[...]))
    loads[2].wait()
    values_t[...] = jnp.transpose(mm(inputs[...], rs_value_ref[...])).astype(BF16)
    position = lax.broadcasted_iota(jnp.int32, (n_lat, rows), 1)
    kept = jnp.logical_or(position < count_ref[0], position >= n_patch)
    for h in rs_heads:
        part = slice(h * RHD, (h + 1) * RHD)
        key = keys_t[part, :]
        centered = key - jnp.mean(key, axis=0, keepdims=True)
        variance = jnp.mean(centered * centered, axis=0, keepdims=True)
        key_h = (centered * lax.rsqrt(variance + EPS)).astype(BF16)
        scores = mm(query_hat[h], key_h) / RHD**0.5
        weights = jnp.where(kept, jnp.exp(scores), 0.0)
        prob = (weights / jnp.sum(weights, axis=-1, keepdims=True)).astype(BF16)
        context_t[part, :] = mm(values_t[part, :], prob, NT).astype(BF16)
    loads[3].wait()
    total = latents_ref[...].astype(F32) + mm(context_t[...], rs_out_ref[...], TN)
    resampled_ref[...] = total
    out_resampled = pltpu.make_async_copy(resampled_ref, resampled_hbm, out_sem.at[2])
    out_resampled.start()
    lat = norm_rows(total).astype(BF16)
    lat_ref[...] = lat
    loads[4].wait()
    key_raw = mm(lat, kw_ref[...])
    key_raw_ref[...] = key_raw
    for h in range(width // HD):
        cols = slice(h * HD, (h + 1) * HD)
        window[REACH, 0, :, cols] = norm_rows(key_raw[:, cols]).astype(BF16)

    pl.semaphore_wait(barrier, len(friends) + n_tp - 1)

    def remote(src, dst, send_sem, recv_sem, to):
        return pltpu.make_async_remote_copy(
            src_ref=src,
            dst_ref=dst,
            send_sem=send_sem,
            recv_sem=recv_sem,
            device_id={"seq": to},
            device_id_type=MESH,
        )

    def pass_on(k_from, k_to, index, to):
        return [
            remote(
                window.at[k_from, g],
                window.at[k_to, g],
                win_send.at[2 * index + g],
                win_recv.at[2 * k_to + g],
                to,
            )
            for g in range(2)
        ]

    pass_a = pass_on(4, 2, 0, ahead)
    pass_b = pass_on(4, 3, 1, partner)
    pass_c = pass_on(2, 0, 2, ahead)
    pass_d0 = pass_on(2, 1, 3, partner)
    pass_d1 = pass_on(2, 3, 3, partner)
    pass_e = pass_on(0, 1, 4, partner)

    def send_own(g):
        pass_a[g].start()

        @pl.when(core == 0)
        def _():
            pass_b[g].start()

    def relay_first(g):
        pass_a[g].wait_recv()
        pass_c[g].start()

        @pl.when(core == 0)
        def _():
            pass_d0[g].start()

        @pl.when(core == 1)
        def _():
            pass_d1[g].start()

    def relay_second(g):
        pass_c[g].wait_recv()

        @pl.when(core == 1)
        def _():
            pass_e[g].start()

    send_own(0)
    loads[5].wait()
    window[REACH, 1] = mm(lat, vw_ref[...]).astype(BF16)
    send_own(1)

    gates = jnp.tanh(gate_ref[...])
    scale = HD**0.5
    loads[6].wait()
    loads[7].wait()
    heads = []
    for h in range(width // HD):
        cols = slice(h * HD, (h + 1) * HD)
        heads.append((h, cols))
        text[:, cols] = norm_rows(q_ref[:, cols]).astype(BF16)
        grad_ctx[:, cols] = (gates[:, h : h + 1] * cot_ref[:, cols].astype(F32)).astype(BF16)
    image = image_ref[...]

    def attend(k):
        match = image == s - REACH + k
        other = jnp.where(match, 0.0, 1.0)
        lat_rows = slice(k * n_lat, (k + 1) * n_lat)
        for h, cols in heads:
            scores = mm(window[k, 0, :, cols], text[:, cols], NT) / scale
            weights = jnp.where(match, jnp.exp(scores), 0.0)
            prob = weights / (jnp.sum(weights, axis=0, keepdims=True) + other)
            low = prob.astype(BF16)
            grad_prob = mm(window[k, 1, :, cols], grad_ctx[:, cols], NT)
            inner = jnp.sum(prob * grad_prob, axis=0, keepdims=True)
            grad_score = (prob * (grad_prob - inner)).astype(BF16)
            probs[h, lat_rows, :] = low
            gscores[h, lat_rows, :] = grad_score
            terms[k, 0, :, cols] = mm(grad_score, text[:, cols]) / scale
            terms[k, 1, :, cols] = mm(low, grad_ctx[:, cols])

    attend(4)
    relay_first(0)
    relay_first(1)
    lat_columns = jnp.transpose(lat_ref[...].astype(F32))
    n_out = n_col // n_seq
    for p in range(XS * YS):
        for c in range(CS):
            start = (p * CS + c) * n_out
            slot_rows = slice(p % YS * n_out, (p % YS + 1) * n_out)
            lat_t[c, p // YS, slot_rows, :] = lat_columns[start : start + n_out]
    attend(2)
    for g in range(2):
        pass_b[g].wait_recv()
    attend(3)
    terms_low[3] = terms[3].astype(BF16)
    relay_second(0)
    relay_second(1)
    attend(0)
    for g in range(2):
        pass_e[g].wait_recv()
    attend(1)
    terms_low[1] = terms[1].astype(BF16)

    def give(k, dst, index, to):
        return [
            remote(
                terms_low.at[k, g],
                dst.at[g],
                back_send.at[2 * index + g],
                back_recv.at[2 * index + g],
                to,
            )
            for g in range(2)
        ]

    give_e = give(1, back_e, 0, partner)
    give_c = give(0, back_c, 1, behind)
    give_d = give(3 - 2 * core, back_d, 2, partner)
    give_b = give(3, back_b, 3, partner)
    give_a = give(2, back_a, 4, behind)

    @pl.when(core == 0)
    def _():
        give_e[0].start()
        give_e[1].start()
        terms_low[0] = terms[0].astype(BF16)

    for g in range(2):

        @pl.when(core == 1)
        def _():
            give_e[g].wait_recv()
            terms_low[0, g] = (terms[0, g] + back_e[g].astype(F32)).astype(BF16)

        give_c[g].start()
        give_d[g].start()

    @pl.when(core == 1)
    def _():
        give_b[0].start()
        give_b[1].start()

    for g in range(2):
        give_d[g].wait_recv()
        near = terms[2, g] + back_d[g].astype(F32)
        give_c[g].wait_recv()
        terms_low[2, g] = (near + back_c[g].astype(F32)).astype(BF16)
        give_a[g].start()

    reduced_ref[...] = terms[REACH]

    @pl.when(core == 0)
    def _():
        for g in range(2):
            give_b[g].wait_recv()
            reduced_ref[g] += back_b[g].astype(F32)

    give_a[0].wait_recv()
    reduced = reduced_ref[0] + back_a[0].astype(F32)
    lows = []
    for h, cols in heads:
        lows.append(norm_back(key_raw_ref[:, cols], reduced[:, cols]).astype(BF16))
    key_low = jnp.concatenate(lows, axis=1)
    give_a[1].wait_recv()
    value_low = (reduced_ref[1] + back_a[1].astype(F32)).astype(BF16)

    for j in range(blocks):
        rows_j = slice(j * HD, (j + 1) * HD)
        part = mm(key_low, kw_ref[rows_j, :], NT) + mm(value_low, vw_ref[rows_j, :], NT)
        parts[j] = part[:half].astype(BF16)
        parts[blocks + j] = part[half:].astype(BF16)

    def red_copy(i):
        to = lax.rem(t + i, n_tp)
        return to, pltpu.make_async_remote_copy(
            src_ref=parts.at[lax.min(to, n_red - 1)],
            dst_ref=parts_in.at[i - 1],
            send_sem=red_send,
            recv_sem=red_recv,
            device_id={"tp": to},
            device_id_type=MESH,
        )

    far_first = sorted(range(1, n_tp), key=lambda i: -min(i, n_tp - i))
    for i in far_first:
        to, copy = red_copy(i)

        @pl.when(to < n_red)
        def _():
            copy.start()

    low = jnp.concatenate([key_low, value_low], axis=1)
    waits = []

    def send(src, dst, index, to):
        copy = remote(src, dst, sems.at[index], recvs.at[index], to)
        copy.start()
        waits.append(copy)
        return copy

    def product(c, xx):
        full = mm(lat_t[c, xx].astype(BF16), low)
        return full.reshape(YS, n_out, 2 * width)

    order = (x_far, x_up, x_dn, x)
    swaps = []
    for i, xx in enumerate(order):
        prod[xx] = product(1 - core, xx).astype(BF16)
        swaps.append(send(prod.at[xx], r1.at[xx], 13 + i, partner))
    hy = YS // 2
    for i, xx in enumerate(order):
        mine = product(core, xx)
        swaps[i].wait_recv()
        a1[xx] = (mine + r1[xx].astype(F32)).astype(BF16)
        if i == 0:
            c1 = send(a1.at[x_far, :hy], r2.at[0], 1, to_xu)
            c2 = send(a1.at[x_far, hy:], r2.at[1], 2, to_xd)
        if i == 1:
            c3 = send(a1.at[x_up, hy:], r3.at[hy:], 3, to_xu)
        if i == 2:
            c4 = send(a1.at[x_dn, :hy], r4.at[:hy], 4, to_xd)

    def all_blocks(ref, send_sem, recv_sem):
        return pltpu.make_async_remote_copy(
            src_ref=ref,
            dst_ref=ref,
            send_sem=send_sem,
            recv_sem=recv_sem,
            device_id={"tp": lax.rem(t + 1, n_tp)},
            device_id_type=MESH,
        )

    slot = lax.min(t, n_red - 1)

    @pl.when(t < n_red)
    def _():
        all_blocks(parts_in, red_send, red_recv).wait_recv()
        total = parts[slot].astype(F32)
        for i in range(n_tp - 1):
            total = total + parts_in[i].astype(F32)
        result[...] = total.astype(BF16)
        for i in far_first:
            pltpu.make_async_remote_copy(
                src_ref=result,
                dst_ref=gathered.at[slot],
                send_sem=all_send,
                recv_sem=all_recv,
                device_id={"tp": lax.rem(t + i, n_tp)},
                device_id_type=MESH,
            ).start()

    c1.wait_recv()
    a1[x_up, :hy] = (a1[x_up, :hy].astype(F32) + r2[0].astype(F32)).astype(BF16)
    c5 = send(a1.at[x_up, :hy], r3.at[:hy], 5, to_xu)
    c2.wait_recv()
    a1[x_dn, hy:] = (a1[x_dn, hy:].astype(F32) + r2[1].astype(F32)).astype(BF16)
    c6 = send(a1.at[x_dn, hy:], r4.at[hy:], 6, to_xd)

    span = (REACH + 1) * n_lat
    for h, cols in heads:
        key_w = window[:, 0, :, cols].reshape(span, HD)
        value_w = window[:, 1, :, cols].reshape(span, HD)
        context = mm(probs[h], value_w, TN)
        att_ref[:, cols] = (gates[:, h : h + 1] * context).astype(BF16)
        grad_hat = mm(gscores[h], key_w, TN) / scale
        gq_ref[:, cols] = norm_back(q_ref[:, cols].astype(F32), grad_hat).astype(BF16)

    out_att = pltpu.make_async_copy(att_ref, att_hbm, out_sem.at[0])
    out_gq = pltpu.make_async_copy(gq_ref, gq_hbm, out_sem.at[1])
    out_att.start()
    out_gq.start()

    c3.wait_recv()
    c4.wait_recv()
    c5.wait_recv()
    c6.wait_recv()
    for yy in range(YS):
        value = a1[x, yy].astype(F32) + r3[yy].astype(F32) + r4[yy].astype(F32)
        a2[yy, 0] = value[:, :width].astype(BF16)
        a2[yy, 1] = value[:, width:].astype(BF16)
    d1 = send(a2.at[y_far, 0], u2.at[0], 7, to_yu)
    d2 = send(a2.at[y_far, 1], u2.at[1], 8, to_yd)
    d3 = send(a2.at[y_up, 1], u3.at[1], 9, to_yu)
    d4 = send(a2.at[y_dn, 0], u4.at[0], 10, to_yd)
    d1.wait_recv()
    a2[y_up, 0] = (a2[y_up, 0].astype(F32) + u2[0].astype(F32)).astype(BF16)
    d5 = send(a2.at[y_up, 0], u3.at[0], 11, to_yu)
    d2.wait_recv()
    a2[y_dn, 1] = (a2[y_dn, 1].astype(F32) + u2[1].astype(F32)).astype(BF16)
    d6 = send(a2.at[y_dn, 1], u4.at[1], 12, to_yd)
    for copy in (d3, d4, d5, d6):
        copy.wait_recv()
    for i in range(2):
        wsum_ref[i] = a2[y, i].astype(F32) + u3[i].astype(F32) + u4[i].astype(F32)

    for copy in waits:
        copy.wait_send()
    for g in range(2):
        for copies in (pass_a, pass_c, pass_d0, give_c, give_d, give_a):
            copies[g].wait_send()

    @pl.when(core == 0)
    def _():
        for g in range(2):
            pass_b[g].wait_send()
            give_e[g].wait_send()

    @pl.when(core == 1)
    def _():
        for g in range(2):
            pass_e[g].wait_send()
            give_b[g].wait_send()

    out_resampled.wait()
    out_att.wait()
    out_gq.wait()

    @pl.when(t < n_red)
    def _():
        all_blocks(parts.at[: n_red - 1], red_send, red_recv).wait_send()
        all_blocks(parts_in, all_send, all_recv).wait_send()
        all_blocks(gathered.at[: n_red - 1], all_send, all_recv).wait_recv()
        gathered[slot] = result[...]

    @pl.when(t >= n_red)
    def _():
        all_blocks(parts, red_send, red_recv).wait_send()
        all_blocks(gathered, all_send, all_recv).wait_recv()


def finish_kernel(
    gathered_hbm,
    resampled_hbm,
    wsum_hbm,
    att_in,
    gq_in,
    att_out,
    gq_out,
    glat_out,
    gk_out,
    gv_out,
    gathered,
    resampled_ref,
    wsum_ref,
    att_ref,
    gq_ref,
    glat_ref,
    in_sem,
    out_sem,
):
    pairs = (
        (gathered_hbm, gathered),
        (resampled_hbm, resampled_ref),
        (wsum_hbm, wsum_ref),
        (att_in, att_ref),
        (gq_in, gq_ref),
    )
    loads = [pltpu.make_async_copy(a, b, in_sem.at[i]) for i, (a, b) in enumerate(pairs)]
    for load in loads:
        load.start()
    stores = []

    def store(src, dst):
        copy = pltpu.make_async_copy(src, dst, out_sem.at[len(stores)])
        copy.start()
        stores.append(copy)

    loads[0].wait()
    loads[1].wait()
    half = gathered.shape[1]
    blocks = gathered.shape[0] // 2
    for k in range(2):
        rows = slice(k * half, (k + 1) * half)
        grad = jnp.concatenate(
            [gathered[k * blocks + j].astype(F32) for j in range(blocks)], axis=1
        )
        glat_ref[rows, :] = norm_back(resampled_ref[rows, :], grad)
        store(glat_ref.at[rows, :], glat_out.at[rows, :])
        if k == 0:
            loads[2].wait()
            store(wsum_ref.at[0], gk_out)
            store(wsum_ref.at[1], gv_out)
            loads[3].wait()
            store(att_ref, att_out)
            loads[4].wait()
            store(gq_ref, gq_out)
    for copy in stores:
        copy.wait()


def on_device(
    queries,
    cotangent,
    gate,
    token_image,
    patches,
    patch_count,
    latents,
    latent_queries,
    rs_key,
    rs_value,
    rs_out,
    key_weight,
    value_weight,
):
    n_seq = lax.axis_size("seq")
    n_tp = lax.axis_size("tp")
    width = key_weight.shape[1]
    tokens = queries.shape[0]
    n_lat, n_col = latents.shape
    n_patch = patches.shape[1]
    inner = latent_queries.shape[1]
    rows = n_patch + n_lat
    heads = width // HD
    span = (REACH + 1) * n_lat
    n_red = 2 * (n_col // HD)
    n_out = n_col // n_seq
    half = n_lat // 2
    vmem = pl.BlockSpec(memory_space=pltpu.VMEM)
    smem = pl.BlockSpec(memory_space=pltpu.SMEM)
    anywhere = pl.BlockSpec(memory_space=pl.ANY)
    dma = pltpu.SemaphoreType.DMA
    slot = (2, n_lat, width)
    bulk = (
        patches[0],
        rs_key,
        rs_value,
        rs_out,
        key_weight,
        value_weight,
        queries,
        cotangent,
    )
    att, gq, resampled, gathered, wsum = pl.pallas_call(
        functools.partial(whole_kernel, n_seq, n_tp, n_red),
        name="whole",
        out_shape=(
            jax.ShapeDtypeStruct((tokens, width), BF16),
            jax.ShapeDtypeStruct((tokens, width), BF16),
            jax.ShapeDtypeStruct((n_lat, n_col), F32),
            jax.ShapeDtypeStruct((n_red, half, HD), BF16),
            jax.ShapeDtypeStruct((2, n_out, width), F32),
        ),
        in_specs=[smem] + [vmem] * 4 + [anywhere] * 8,
        out_specs=(anywhere,) * 3 + (vmem,) * 2,
        scratch_shapes=[
            pltpu.VMEM((tokens, width), BF16),
            pltpu.VMEM((tokens, width), BF16),
            pltpu.VMEM((n_lat, n_col), F32),
        ]
        + [pltpu.VMEM(a.shape, a.dtype) for a in bulk]
        + [
            pltpu.VMEM((rows, n_col), BF16),
            pltpu.VMEM((inner // RHD, n_lat, RHD), BF16),
            pltpu.VMEM((inner, rows), F32),
            pltpu.VMEM((inner, rows), BF16),
            pltpu.VMEM((inner, n_lat), BF16),
            pltpu.VMEM((n_lat, n_col), BF16),
            pltpu.VMEM((CS, XS, YS * n_out, n_lat), F32),
            pltpu.VMEM((n_lat, width), F32),
            pltpu.VMEM((REACH + 1,) + slot, BF16),
            pltpu.VMEM((tokens, width), BF16),
            pltpu.VMEM((tokens, width), BF16),
            pltpu.VMEM((heads, span, tokens), BF16),
            pltpu.VMEM((heads, span, tokens), BF16),
            pltpu.VMEM((REACH + 1,) + slot, F32),
            pltpu.VMEM((REACH,) + slot, BF16),
            pltpu.VMEM(slot, BF16),
            pltpu.VMEM(slot, BF16),
            pltpu.VMEM(slot, BF16),
            pltpu.VMEM(slot, BF16),
            pltpu.VMEM(slot, BF16),
            pltpu.VMEM(slot, F32),
            pltpu.VMEM((n_red, half, HD), BF16),
            pltpu.VMEM((n_tp - 1, half, HD), BF16),
            pltpu.VMEM((half, HD), BF16),
            pltpu.VMEM((XS, YS, n_out, 2 * width), BF16),
            pltpu.VMEM((XS, YS, n_out, 2 * width), BF16),
            pltpu.VMEM((XS, YS, n_out, 2 * width), BF16),
            pltpu.VMEM((2, YS // 2, n_out, 2 * width), BF16),
            pltpu.VMEM((YS, n_out, 2 * width), BF16),
            pltpu.VMEM((YS, n_out, 2 * width), BF16),
            pltpu.VMEM((YS, 2, n_out, width), BF16),
            pltpu.VMEM((2, n_out, width), BF16),
            pltpu.VMEM((2, n_out, width), BF16),
            pltpu.VMEM((2, n_out, width), BF16),
            dma((3,)),
            dma((8,)),
            dma((10,)),
            dma((8,)),
            dma((10,)),
            dma((10,)),
            dma(()),
            dma(()),
            dma(()),
            dma(()),
            dma((17,)),
            dma((17,)),
        ],
        compiler_params=pltpu.CompilerParams(collective_id=0, has_side_effects=True),
    )(
        patch_count,
        latents,
        latent_queries,
        gate.reshape(1, heads),
        token_image.reshape(1, tokens),
        *bulk,
    )
    attended, grad_query, grad_latents, grad_key_weight, grad_value_weight = pl.pallas_call(
        finish_kernel,
        name="finish",
        out_shape=(
            jax.ShapeDtypeStruct((tokens, width), BF16),
            jax.ShapeDtypeStruct((tokens, width), BF16),
            jax.ShapeDtypeStruct((n_lat, n_col), F32),
            jax.ShapeDtypeStruct((n_out, width), F32),
            jax.ShapeDtypeStruct((n_out, width), F32),
        ),
        in_specs=[anywhere] * 5,
        out_specs=(anywhere,) * 5,
        scratch_shapes=[
            pltpu.VMEM(a.shape, a.dtype) for a in (gathered, resampled, wsum, att, gq, resampled)
        ]
        + [dma((5,)), dma((6,))],
    )(gathered, resampled, wsum, att, gq)
    return (attended, grad_query, grad_latents[None], grad_key_weight, grad_value_weight)


def solution(mesh):
    placed = (
        P("seq", "tp"),
        P("seq", "tp"),
        P("tp"),
        P("seq"),
        P("seq", None, None),
        P("seq"),
        P(),
        P(),
        P(),
        P(),
        P(),
        P(None, "tp"),
        P(None, "tp"),
    )
    return jax.shard_map(
        on_device,
        mesh=mesh,
        in_specs=placed,
        out_specs=(
            P("seq", "tp"),
            P("seq", "tp"),
            P("seq", None, None),
            P("seq", "tp"),
            P("seq", "tp"),
        ),
        check_vma=False,
    )
```

```python
import functools

import jax
import jax.numpy as jnp
from jax import lax
from jax.experimental import pallas as pl
from jax.experimental.pallas import tpu as pltpu
from jax.sharding import PartitionSpec as P

HD = 128
RHD = 96
REACH = 4
EPS = 1e-05
XS, YS, CS = 4, 4, 2
MESH = pl.DeviceIdType.MESH
F32 = jnp.float32
BF16 = jnp.bfloat16
NT = (((1,), (1,)), ((), ()))
TN = (((0,), (0,)), ((), ()))


def mm(a, b, dims=(((1,), (0,)), ((), ()))):
    return lax.dot_general(a, b, dims, preferred_element_type=F32)


def norm_stats(matrix):
    average = jnp.mean(matrix, axis=-1, keepdims=True)
    centered = matrix - average
    variance = jnp.mean(centered * centered, axis=-1, keepdims=True)
    inverse = lax.rsqrt(variance + EPS)
    return centered * inverse, inverse


def norm_rows(matrix):
    return norm_stats(matrix.astype(F32))[0]


def norm_back(matrix, incoming):
    normed, inverse = norm_stats(matrix)
    first_mean = jnp.mean(incoming, axis=-1, keepdims=True)
    second_mean = jnp.mean(incoming * normed, axis=-1, keepdims=True)
    return inverse * (incoming - first_mean - normed * second_mean)


def whole_kernel(
    n_seq,
    n_tp,
    n_red,
    count_ref,
    latents_ref,
    lq_ref,
    gate_ref,
    image_ref,
    patches_hbm,
    rs_key_hbm,
    rs_value_hbm,
    rs_out_hbm,
    kw_hbm,
    vw_hbm,
    q_hbm,
    cot_hbm,
    att_hbm,
    gq_hbm,
    resampled_hbm,
    gathered,
    wsum_ref,
    att_ref,
    gq_ref,
    resampled_ref,
    patches_ref,
    rs_key_ref,
    rs_value_ref,
    rs_out_ref,
    kw_ref,
    vw_ref,
    q_ref,
    cot_ref,
    inputs,
    query_hat,
    keys_t,
    values_t,
    context_t,
    lat_ref,
    lat_t,
    key_raw_ref,
    window,
    text,
    grad_ctx,
    probs,
    gscores,
    terms,
    terms_low,
    back_e,
    back_c,
    back_d,
    back_b,
    back_a,
    reduced_ref,
    parts,
    parts_in,
    result,
    prod,
    r1,
    a1,
    r2,
    r3,
    r4,
    a2,
    u2,
    u3,
    u4,
    out_sem,
    load_sem,
    win_send,
    win_recv,
    back_send,
    back_recv,
    red_send,
    red_recv,
    all_send,
    all_recv,
    sems,
    recvs,
):
    s = lax.axis_index("seq")
    t = lax.axis_index("tp")
    width = kw_ref.shape[1]
    n_lat, n_col = lat_ref.shape
    half = n_lat // 2
    blocks = n_col // HD
    tokens = q_ref.shape[0]
    core = lax.rem(s, CS)
    chip = lax.div(s, CS)
    y = lax.rem(chip, YS)
    x = lax.div(chip, YS)

    def seq_of(xx, yy, cc):
        return (xx * YS + yy) * CS + cc

    partner = seq_of(x, y, 1 - core)
    ahead, behind = lax.rem(s + CS, n_seq), lax.rem(s + n_seq - CS, n_seq)
    x_up, x_dn, x_far = lax.rem(x + 1, XS), lax.rem(x + XS - 1, XS), lax.rem(x + 2, XS)
    y_up, y_dn, y_far = lax.rem(y + 1, YS), lax.rem(y + YS - 1, YS), lax.rem(y + 2, YS)
    to_xu, to_xd = seq_of(x_up, y, core), seq_of(x_dn, y, core)
    to_yu, to_yd = seq_of(x, y_up, core), seq_of(x, y_dn, core)

    loads = []
    for i, (src, dst) in enumerate(
        (
            (patches_hbm, patches_ref),
            (rs_key_hbm, rs_key_ref),
            (rs_value_hbm, rs_value_ref),
            (rs_out_hbm, rs_out_ref),
            (kw_hbm, kw_ref),
            (vw_hbm, vw_ref),
            (q_hbm, q_ref),
            (cot_hbm, cot_ref),
        )
    ):
        load = pltpu.make_async_copy(src, dst, load_sem.at[i])
        load.start()
        loads.append(load)

    barrier = pltpu.get_barrier_semaphore()
    friends = [partner, ahead, behind, to_xu, to_xd, to_yu, to_yd]
    for other in friends:
        pl.semaphore_signal(barrier, inc=1, device_id={"seq": other}, device_id_type=MESH)
    for i in range(1, n_tp):
        pl.semaphore_signal(
            barrier, inc=1, device_id={"tp": lax.rem(t + i, n_tp)}, device_id_type=MESH
        )

    n_patch = patches_ref.shape[0]
    rows = n_patch + n_lat
    inputs[n_patch:, :] = norm_rows(latents_ref[...]).astype(BF16)
    queries = lq_ref[...].astype(F32)
    rs_heads = range(lq_ref.shape[1] // RHD)
    for h in rs_heads:
        query_hat[h] = norm_rows(queries[:, h * RHD : (h + 1) * RHD]).astype(BF16)
    loads[0].wait()
    for r in range(0, n_patch, 64):
        inputs[r : r + 64, :] = norm_rows(patches_ref[r : r + 64, :]).astype(BF16)
    loads[1].wait()
    keys_t[...] = jnp.transpose(mm(inputs[...], rs_key_ref[...]))
    loads[2].wait()
    values_t[...] = jnp.transpose(mm(inputs[...], rs_value_ref[...])).astype(BF16)
    position = lax.broadcasted_iota(jnp.int32, (n_lat, rows), 1)
    kept = jnp.logical_or(position < count_ref[0], position >= n_patch)
    for h in rs_heads:
        part = slice(h * RHD, (h + 1) * RHD)
        key = keys_t[part, :]
        centered = key - jnp.mean(key, axis=0, keepdims=True)
        variance = jnp.mean(centered * centered, axis=0, keepdims=True)
        key_h = (centered * lax.rsqrt(variance + EPS)).astype(BF16)
        scores = mm(query_hat[h], key_h) / RHD**0.5
        weights = jnp.where(kept, jnp.exp(scores), 0.0)
        prob = (weights / jnp.sum(weights, axis=-1, keepdims=True)).astype(BF16)
        context_t[part, :] = mm(values_t[part, :], prob, NT).astype(BF16)
    loads[3].wait()
    total = latents_ref[...].astype(F32) + mm(context_t[...], rs_out_ref[...], TN)
    resampled_ref[...] = total
    out_resampled = pltpu.make_async_copy(resampled_ref, resampled_hbm, out_sem.at[2])
    out_resampled.start()
    lat = norm_rows(total).astype(BF16)
    lat_ref[...] = lat
    loads[4].wait()
    key_raw = mm(lat, kw_ref[...])
    key_raw_ref[...] = key_raw
    for h in range(width // HD):
        cols = slice(h * HD, (h + 1) * HD)
        window[REACH, 0, :, cols] = norm_rows(key_raw[:, cols]).astype(BF16)

    pl.semaphore_wait(barrier, len(friends) + n_tp - 1)

    def remote(src, dst, send_sem, recv_sem, to):
        return pltpu.make_async_remote_copy(
            src_ref=src,
            dst_ref=dst,
            send_sem=send_sem,
            recv_sem=recv_sem,
            device_id={"seq": to},
            device_id_type=MESH,
        )

    def pass_on(k_from, k_to, index, to):
        return [
            remote(
                window.at[k_from, g],
                window.at[k_to, g],
                win_send.at[2 * index + g],
                win_recv.at[2 * k_to + g],
                to,
            )
            for g in range(2)
        ]

    pass_a = pass_on(4, 2, 0, ahead)
    pass_b = pass_on(4, 3, 1, partner)
    pass_c = pass_on(2, 0, 2, ahead)
    pass_d0 = pass_on(2, 1, 3, partner)
    pass_d1 = pass_on(2, 3, 3, partner)
    pass_e = pass_on(0, 1, 4, partner)

    def send_own(g):
        pass_a[g].start()

        @pl.when(core == 0)
        def _():
            pass_b[g].start()

    def relay_first(g):
        pass_a[g].wait_recv()
        pass_c[g].start()

        @pl.when(core == 0)
        def _():
            pass_d0[g].start()

        @pl.when(core == 1)
        def _():
            pass_d1[g].start()

    def relay_second(g):
        pass_c[g].wait_recv()

        @pl.when(core == 1)
        def _():
            pass_e[g].start()

    send_own(0)
    loads[5].wait()
    window[REACH, 1] = mm(lat, vw_ref[...]).astype(BF16)
    send_own(1)

    gates = jnp.tanh(gate_ref[...])
    scale = HD**0.5
    loads[6].wait()
    loads[7].wait()
    heads = []
    for h in range(width // HD):
        cols = slice(h * HD, (h + 1) * HD)
        heads.append((h, cols))
        text[:, cols] = norm_rows(q_ref[:, cols]).astype(BF16)
        grad_ctx[:, cols] = (gates[:, h : h + 1] * cot_ref[:, cols].astype(F32)).astype(BF16)
    image = image_ref[...]

    def attend(k):
        match = image == s - REACH + k
        other = jnp.where(match, 0.0, 1.0)
        lat_rows = slice(k * n_lat, (k + 1) * n_lat)
        for h, cols in heads:
            scores = mm(window[k, 0, :, cols], text[:, cols], NT) / scale
            weights = jnp.where(match, jnp.exp(scores), 0.0)
            prob = weights / (jnp.sum(weights, axis=0, keepdims=True) + other)
            low = prob.astype(BF16)
            grad_prob = mm(window[k, 1, :, cols], grad_ctx[:, cols], NT)
            inner = jnp.sum(prob * grad_prob, axis=0, keepdims=True)
            grad_score = (prob * (grad_prob - inner)).astype(BF16)
            probs[h, lat_rows, :] = low
            gscores[h, lat_rows, :] = grad_score
            terms[k, 0, :, cols] = mm(grad_score, text[:, cols]) / scale
            terms[k, 1, :, cols] = mm(low, grad_ctx[:, cols])

    attend(4)
    relay_first(0)
    relay_first(1)
    lat_columns = jnp.transpose(lat_ref[...].astype(F32))
    n_out = n_col // n_seq
    for p in range(XS * YS):
        for c in range(CS):
            start = (p * CS + c) * n_out
            slot_rows = slice(p % YS * n_out, (p % YS + 1) * n_out)
            lat_t[c, p // YS, slot_rows, :] = lat_columns[start : start + n_out]
    attend(2)
    for g in range(2):
        pass_b[g].wait_recv()
    attend(3)
    terms_low[3] = terms[3].astype(BF16)
    relay_second(0)
    relay_second(1)
    attend(0)
    for g in range(2):
        pass_e[g].wait_recv()
    attend(1)
    terms_low[1] = terms[1].astype(BF16)

    def give(k, dst, index, to):
        return [
            remote(
                terms_low.at[k, g],
                dst.at[g],
                back_send.at[2 * index + g],
                back_recv.at[2 * index + g],
                to,
            )
            for g in range(2)
        ]

    give_e = give(1, back_e, 0, partner)
    give_c = give(0, back_c, 1, behind)
    give_d = give(3 - 2 * core, back_d, 2, partner)
    give_b = give(3, back_b, 3, partner)
    give_a = give(2, back_a, 4, behind)

    @pl.when(core == 0)
    def _():
        give_e[0].start()
        give_e[1].start()
        terms_low[0] = terms[0].astype(BF16)

    for g in range(2):

        @pl.when(core == 1)
        def _():
            give_e[g].wait_recv()
            terms_low[0, g] = (terms[0, g] + back_e[g].astype(F32)).astype(BF16)

        give_c[g].start()
        give_d[g].start()

    @pl.when(core == 1)
    def _():
        give_b[0].start()
        give_b[1].start()

    for g in range(2):
        give_d[g].wait_recv()
        near = terms[2, g] + back_d[g].astype(F32)
        give_c[g].wait_recv()
        terms_low[2, g] = (near + back_c[g].astype(F32)).astype(BF16)
        give_a[g].start()

    reduced_ref[...] = terms[REACH]

    @pl.when(core == 0)
    def _():
        for g in range(2):
            give_b[g].wait_recv()
            reduced_ref[g] += back_b[g].astype(F32)

    give_a[0].wait_recv()
    reduced = reduced_ref[0] + back_a[0].astype(F32)
    lows = []
    for h, cols in heads:
        lows.append(norm_back(key_raw_ref[:, cols], reduced[:, cols]).astype(BF16))
    key_low = jnp.concatenate(lows, axis=1)
    give_a[1].wait_recv()
    value_low = (reduced_ref[1] + back_a[1].astype(F32)).astype(BF16)

    for j in range(blocks):
        rows_j = slice(j * HD, (j + 1) * HD)
        part = mm(key_low, kw_ref[rows_j, :], NT) + mm(value_low, vw_ref[rows_j, :], NT)
        parts[j] = part[:half].astype(BF16)
        parts[blocks + j] = part[half:].astype(BF16)

    def red_copy(i):
        to = lax.rem(t + i, n_tp)
        return to, pltpu.make_async_remote_copy(
            src_ref=parts.at[lax.min(to, n_red - 1)],
            dst_ref=parts_in.at[i - 1],
            send_sem=red_send,
            recv_sem=red_recv,
            device_id={"tp": to},
            device_id_type=MESH,
        )

    far_first = sorted(range(1, n_tp), key=lambda i: -min(i, n_tp - i))
    for i in far_first:
        to, copy = red_copy(i)

        @pl.when(to < n_red)
        def _():
            copy.start()

    low = jnp.concatenate([key_low, value_low], axis=1)
    waits = []

    def send(src, dst, index, to):
        copy = remote(src, dst, sems.at[index], recvs.at[index], to)
        copy.start()
        waits.append(copy)
        return copy

    def product(c, xx):
        full = mm(lat_t[c, xx].astype(BF16), low)
        return full.reshape(YS, n_out, 2 * width)

    order = (x_far, x_up, x_dn, x)
    swaps = []
    for i, xx in enumerate(order):
        prod[xx] = product(1 - core, xx).astype(BF16)
        swaps.append(send(prod.at[xx], r1.at[xx], 13 + i, partner))
    hy = YS // 2
    for i, xx in enumerate(order):
        mine = product(core, xx)
        swaps[i].wait_recv()
        a1[xx] = (mine + r1[xx].astype(F32)).astype(BF16)
        if i == 0:
            c1 = send(a1.at[x_far, :hy], r2.at[0], 1, to_xu)
            c2 = send(a1.at[x_far, hy:], r2.at[1], 2, to_xd)
        if i == 1:
            c3 = send(a1.at[x_up, hy:], r3.at[hy:], 3, to_xu)
        if i == 2:
            c4 = send(a1.at[x_dn, :hy], r4.at[:hy], 4, to_xd)

    def all_blocks(ref, send_sem, recv_sem):
        return pltpu.make_async_remote_copy(
            src_ref=ref,
            dst_ref=ref,
            send_sem=send_sem,
            recv_sem=recv_sem,
            device_id={"tp": lax.rem(t + 1, n_tp)},
            device_id_type=MESH,
        )

    slot = lax.min(t, n_red - 1)

    def reduce_blocks():
        all_blocks(parts_in, red_send, red_recv).wait_recv()
        total = parts[slot].astype(F32)
        for i in range(n_tp - 1):
            total = total + parts_in[i].astype(F32)
        result[...] = total.astype(BF16)
        for i in far_first:
            pltpu.make_async_remote_copy(
                src_ref=result,
                dst_ref=gathered.at[slot],
                send_sem=all_send,
                recv_sem=all_recv,
                device_id={"tp": lax.rem(t + i, n_tp)},
                device_id_type=MESH,
            ).start()

    early = n_tp // 2

    @pl.when(jnp.logical_and(t >= early, t < n_red))
    def _():
        reduce_blocks()

    c1.wait_recv()
    a1[x_up, :hy] = (a1[x_up, :hy].astype(F32) + r2[0].astype(F32)).astype(BF16)
    c5 = send(a1.at[x_up, :hy], r3.at[:hy], 5, to_xu)
    c2.wait_recv()
    a1[x_dn, hy:] = (a1[x_dn, hy:].astype(F32) + r2[1].astype(F32)).astype(BF16)
    c6 = send(a1.at[x_dn, hy:], r4.at[hy:], 6, to_xd)

    span = (REACH + 1) * n_lat
    for h, cols in heads:
        key_w = window[:, 0, :, cols].reshape(span, HD)
        value_w = window[:, 1, :, cols].reshape(span, HD)
        context = mm(probs[h], value_w, TN)
        att_ref[:, cols] = (gates[:, h : h + 1] * context).astype(BF16)
        grad_hat = mm(gscores[h], key_w, TN) / scale
        gq_ref[:, cols] = norm_back(q_ref[:, cols].astype(F32), grad_hat).astype(BF16)

    out_att = pltpu.make_async_copy(att_ref, att_hbm, out_sem.at[0])
    out_gq = pltpu.make_async_copy(gq_ref, gq_hbm, out_sem.at[1])
    out_att.start()
    out_gq.start()

    c3.wait_recv()
    c4.wait_recv()
    c5.wait_recv()
    c6.wait_recv()
    for yy in range(YS):
        value = a1[x, yy].astype(F32) + r3[yy].astype(F32) + r4[yy].astype(F32)
        a2[yy, 0] = value[:, :width].astype(BF16)
        a2[yy, 1] = value[:, width:].astype(BF16)
    d1 = send(a2.at[y_far, 0], u2.at[0], 7, to_yu)
    d2 = send(a2.at[y_far, 1], u2.at[1], 8, to_yd)
    d3 = send(a2.at[y_up, 1], u3.at[1], 9, to_yu)
    d4 = send(a2.at[y_dn, 0], u4.at[0], 10, to_yd)

    @pl.when(t < early)
    def _():
        reduce_blocks()

    d1.wait_recv()
    a2[y_up, 0] = (a2[y_up, 0].astype(F32) + u2[0].astype(F32)).astype(BF16)
    d5 = send(a2.at[y_up, 0], u3.at[0], 11, to_yu)
    d2.wait_recv()
    a2[y_dn, 1] = (a2[y_dn, 1].astype(F32) + u2[1].astype(F32)).astype(BF16)
    d6 = send(a2.at[y_dn, 1], u4.at[1], 12, to_yd)
    for copy in (d3, d4, d5, d6):
        copy.wait_recv()
    for i in range(2):
        wsum_ref[i] = a2[y, i].astype(F32) + u3[i].astype(F32) + u4[i].astype(F32)

    for copy in waits:
        copy.wait_send()
    for g in range(2):
        for copies in (pass_a, pass_c, pass_d0, give_c, give_d, give_a):
            copies[g].wait_send()

    @pl.when(core == 0)
    def _():
        for g in range(2):
            pass_b[g].wait_send()
            give_e[g].wait_send()

    @pl.when(core == 1)
    def _():
        for g in range(2):
            pass_e[g].wait_send()
            give_b[g].wait_send()

    out_resampled.wait()
    out_att.wait()
    out_gq.wait()

    @pl.when(t < n_red)
    def _():
        all_blocks(parts.at[: n_red - 1], red_send, red_recv).wait_send()
        all_blocks(parts_in, all_send, all_recv).wait_send()
        all_blocks(gathered.at[: n_red - 1], all_send, all_recv).wait_recv()
        gathered[slot] = result[...]

    @pl.when(t >= n_red)
    def _():
        all_blocks(parts, red_send, red_recv).wait_send()
        all_blocks(gathered, all_send, all_recv).wait_recv()


def finish_kernel(
    gathered_hbm,
    resampled_hbm,
    wsum_hbm,
    att_in,
    gq_in,
    att_out,
    gq_out,
    glat_out,
    gk_out,
    gv_out,
    gathered,
    resampled_ref,
    wsum_ref,
    att_ref,
    gq_ref,
    glat_ref,
    in_sem,
    out_sem,
):
    pairs = (
        (gathered_hbm, gathered),
        (resampled_hbm, resampled_ref),
        (wsum_hbm, wsum_ref),
        (att_in, att_ref),
        (gq_in, gq_ref),
    )
    loads = [pltpu.make_async_copy(a, b, in_sem.at[i]) for i, (a, b) in enumerate(pairs)]
    for load in loads:
        load.start()
    stores = []

    def store(src, dst):
        copy = pltpu.make_async_copy(src, dst, out_sem.at[len(stores)])
        copy.start()
        stores.append(copy)

    loads[0].wait()
    loads[1].wait()
    half = gathered.shape[1]
    blocks = gathered.shape[0] // 2
    for k in range(2):
        rows = slice(k * half, (k + 1) * half)
        grad = jnp.concatenate(
            [gathered[k * blocks + j].astype(F32) for j in range(blocks)], axis=1
        )
        glat_ref[rows, :] = norm_back(resampled_ref[rows, :], grad)
        store(glat_ref.at[rows, :], glat_out.at[rows, :])
        if k == 0:
            loads[2].wait()
            store(wsum_ref.at[0], gk_out)
            store(wsum_ref.at[1], gv_out)
            loads[3].wait()
            store(att_ref, att_out)
            loads[4].wait()
            store(gq_ref, gq_out)
    for copy in stores:
        copy.wait()


def on_device(
    queries,
    cotangent,
    gate,
    token_image,
    patches,
    patch_count,
    latents,
    latent_queries,
    rs_key,
    rs_value,
    rs_out,
    key_weight,
    value_weight,
):
    n_seq = lax.axis_size("seq")
    n_tp = lax.axis_size("tp")
    width = key_weight.shape[1]
    tokens = queries.shape[0]
    n_lat, n_col = latents.shape
    n_patch = patches.shape[1]
    inner = latent_queries.shape[1]
    rows = n_patch + n_lat
    heads = width // HD
    span = (REACH + 1) * n_lat
    n_red = 2 * (n_col // HD)
    n_out = n_col // n_seq
    half = n_lat // 2
    vmem = pl.BlockSpec(memory_space=pltpu.VMEM)
    smem = pl.BlockSpec(memory_space=pltpu.SMEM)
    anywhere = pl.BlockSpec(memory_space=pl.ANY)
    dma = pltpu.SemaphoreType.DMA
    slot = (2, n_lat, width)
    bulk = (
        patches[0],
        rs_key,
        rs_value,
        rs_out,
        key_weight,
        value_weight,
        queries,
        cotangent,
    )
    att, gq, resampled, gathered, wsum = pl.pallas_call(
        functools.partial(whole_kernel, n_seq, n_tp, n_red),
        name="whole",
        out_shape=(
            jax.ShapeDtypeStruct((tokens, width), BF16),
            jax.ShapeDtypeStruct((tokens, width), BF16),
            jax.ShapeDtypeStruct((n_lat, n_col), F32),
            jax.ShapeDtypeStruct((n_red, half, HD), BF16),
            jax.ShapeDtypeStruct((2, n_out, width), F32),
        ),
        in_specs=[smem] + [vmem] * 4 + [anywhere] * 8,
        out_specs=(anywhere,) * 3 + (vmem,) * 2,
        scratch_shapes=[
            pltpu.VMEM((tokens, width), BF16),
            pltpu.VMEM((tokens, width), BF16),
            pltpu.VMEM((n_lat, n_col), F32),
        ]
        + [pltpu.VMEM(a.shape, a.dtype) for a in bulk]
        + [
            pltpu.VMEM((rows, n_col), BF16),
            pltpu.VMEM((inner // RHD, n_lat, RHD), BF16),
            pltpu.VMEM((inner, rows), F32),
            pltpu.VMEM((inner, rows), BF16),
            pltpu.VMEM((inner, n_lat), BF16),
            pltpu.VMEM((n_lat, n_col), BF16),
            pltpu.VMEM((CS, XS, YS * n_out, n_lat), F32),
            pltpu.VMEM((n_lat, width), F32),
            pltpu.VMEM((REACH + 1,) + slot, BF16),
            pltpu.VMEM((tokens, width), BF16),
            pltpu.VMEM((tokens, width), BF16),
            pltpu.VMEM((heads, span, tokens), BF16),
            pltpu.VMEM((heads, span, tokens), BF16),
            pltpu.VMEM((REACH + 1,) + slot, F32),
            pltpu.VMEM((REACH,) + slot, BF16),
            pltpu.VMEM(slot, BF16),
            pltpu.VMEM(slot, BF16),
            pltpu.VMEM(slot, BF16),
            pltpu.VMEM(slot, BF16),
            pltpu.VMEM(slot, BF16),
            pltpu.VMEM(slot, F32),
            pltpu.VMEM((n_red, half, HD), BF16),
            pltpu.VMEM((n_tp - 1, half, HD), BF16),
            pltpu.VMEM((half, HD), BF16),
            pltpu.VMEM((XS, YS, n_out, 2 * width), BF16),
            pltpu.VMEM((XS, YS, n_out, 2 * width), BF16),
            pltpu.VMEM((XS, YS, n_out, 2 * width), BF16),
            pltpu.VMEM((2, YS // 2, n_out, 2 * width), BF16),
            pltpu.VMEM((YS, n_out, 2 * width), BF16),
            pltpu.VMEM((YS, n_out, 2 * width), BF16),
            pltpu.VMEM((YS, 2, n_out, width), BF16),
            pltpu.VMEM((2, n_out, width), BF16),
            pltpu.VMEM((2, n_out, width), BF16),
            pltpu.VMEM((2, n_out, width), BF16),
            dma((3,)),
            dma((8,)),
            dma((10,)),
            dma((8,)),
            dma((10,)),
            dma((10,)),
            dma(()),
            dma(()),
            dma(()),
            dma(()),
            dma((17,)),
            dma((17,)),
        ],
        compiler_params=pltpu.CompilerParams(collective_id=0, has_side_effects=True),
    )(
        patch_count,
        latents,
        latent_queries,
        gate.reshape(1, heads),
        token_image.reshape(1, tokens),
        *bulk,
    )
    attended, grad_query, grad_latents, grad_key_weight, grad_value_weight = pl.pallas_call(
        finish_kernel,
        name="finish",
        out_shape=(
            jax.ShapeDtypeStruct((tokens, width), BF16),
            jax.ShapeDtypeStruct((tokens, width), BF16),
            jax.ShapeDtypeStruct((n_lat, n_col), F32),
            jax.ShapeDtypeStruct((n_out, width), F32),
            jax.ShapeDtypeStruct((n_out, width), F32),
        ),
        in_specs=[anywhere] * 5,
        out_specs=(anywhere,) * 5,
        scratch_shapes=[
            pltpu.VMEM(a.shape, a.dtype) for a in (gathered, resampled, wsum, att, gq, resampled)
        ]
        + [dma((5,)), dma((6,))],
    )(gathered, resampled, wsum, att, gq)
    return (attended, grad_query, grad_latents[None], grad_key_weight, grad_value_weight)


def solution(mesh):
    placed = (
        P("seq", "tp"),
        P("seq", "tp"),
        P("tp"),
        P("seq"),
        P("seq", None, None),
        P("seq"),
        P(),
        P(),
        P(),
        P(),
        P(),
        P(None, "tp"),
        P(None, "tp"),
    )
    return jax.shard_map(
        on_device,
        mesh=mesh,
        in_specs=placed,
        out_specs=(
            P("seq", "tp"),
            P("seq", "tp"),
            P("seq", None, None),
            P("seq", "tp"),
            P("seq", "tp"),
        ),
        check_vma=False,
    )
```
